32 devices in a mesh: cells: 16 (over z, y, core), waves: 2 (over x).
Axes of the slice: x: 2, y: 2, z: 4, core: 2. Of those that a mesh axis runs over, the one named last changes fastest.
Arguments:
- features: bfloat16 [32768, 512], P('cells', 'waves'), may hold values from -6 to 6
- positions: float32 [3, 32768], P(None, 'cells'), may hold values from 0 to 256, as said below
- occupancy: int32 [256], P('cells'), may hold values from 1 to 128, as said below
- neighbours: int32 [256, 3], P('cells'), may hold values from -2 to 2, as said below
- wavevectors: float32 [3, 4096], P(None, 'waves'), may hold values from -1 to 1
- filters: float32 [4096, 512], P('waves'), may hold values from -6 to 6
- falloffs: float32 [4], replicated, may hold values from 0.05 to 2
- mixing: float32 [4, 512], replicated, may hold values from -2 to 2
- norm_gain: float32 [512], replicated, may hold values from 0.5 to 1.5
- in_weight: bfloat16 [512, 1024], P(None, 'waves'), may hold values from -0.25 to 0.25
- out_weight: bfloat16 [1024, 512], P('waves'), may hold values from -0.1875 to 0.1875
Outputs:
- result: bfloat16 [32768, 512], P('cells', 'waves')
The draws below stay inside these ranges and needn't reach their ends.
Inputs may be any that keep to these rules, and one draw needn't show every extreme that they name: `occupancy`: the atoms of a cell fill its first slots; the last cell is full. `neighbours`: each row holds 3 distinct offsets; cell c interacts with cells c + offset modulo 256. `positions`: the first coordinate of an atom in cell c lies in [c, c + 1]; the other two lie in [0, 3].
All inputs are finite; a program needn't handle non-finite values.
Results may differ from the reference program's by a relative error of at most 0.009.
Values may be sent and summed in bfloat16 or wider, within the bound.
No kernel may reach another device: no remote copies, remote signals or barrier semaphores. Data moves between devices by JAX's collectives and lax.ppermute only.
A program may use at most 128 MiB of HBM per device.

```python
import math
import jax
import jax.numpy as jnp
from jax import lax

F = 512
H = 1024
K = 4096
G = 4
CAP = 128
NB = 3
HW = 2
NCELLS = 256
ATOMS = 32768


def draw_positions(key, part):
    key_along, key_across = jax.random.split(key)
    along = jax.random.uniform(key_along, (ATOMS,), jnp.float32)
    cell_number = (jnp.arange(ATOMS, dtype=jnp.int32) // CAP).astype(jnp.float32)
    across = jax.random.uniform(key_across, (2, ATOMS), jnp.float32) * 3.0
    return jnp.concatenate([(cell_number + along)[None, :], across], axis=0)


def draw_occupancy(key, part):
    key_fill, key_counts = jax.random.split(key)
    fill_level = jax.random.randint(key_fill, (), 102, 257)
    cell_number = jnp.arange(NCELLS, dtype=jnp.int32)
    ramp = CAP // 3 + (CAP - CAP // 3) * cell_number // max(NCELLS - 1, 1)
    ceiling = jnp.maximum(ramp * fill_level // 256, 1)
    floor_count = jnp.maximum(3 * ceiling // 4, 1)
    drawn = jax.random.randint(key_counts, (NCELLS,), floor_count, ceiling + 1)
    return drawn.at[NCELLS - 1].set(CAP).astype(jnp.int32)


def draw_neighbours(key, part):
    span_count = 2 * HW + 1
    scores = jax.random.randint(key, (NCELLS, span_count), 0, 4096) * span_count + jnp.arange(span_count, dtype=jnp.int32)[None, :]
    ranked = jnp.argsort(scores, axis=1)
    return (ranked[:, :NB] - HW).astype(jnp.int32)


def level_of(own_key, extent, shards, low, high):
    loudness, own = 1.0, jax.random.fold_in(own_key, 6)
    for position, blocks in shards:
        steps = jnp.exp(jax.random.uniform(jax.random.fold_in(own, position), (blocks,), jnp.float32, low / len(shards), high / len(shards)))
        loudness = loudness * jnp.repeat(steps, extent[position] // blocks).reshape([-1 if axis == position else 1 for axis in range(len(extent))])
    return loudness


def normal_values(key, extent, width, reach, cuts=(), held_as=jnp.bfloat16):
    array = jax.random.normal(key, extent, jnp.float32) * width
    if len(cuts) > 0:
        array = level_of(key, extent, cuts, -0.22, 0.18) * array
    return jnp.clip(array, min=-reach, max=reach).astype(held_as)


def setup_inputs(seed: int = 0) -> dict:
    arg_keys = jax.random.split(jax.random.key(seed), 12)
    features = normal_values(arg_keys[0], (ATOMS, F), 1.0, 6.0, ((0, 16), (1, 2)))
    positions = draw_positions(jax.random.fold_in(arg_keys[11], 71), 0)
    occupancy = draw_occupancy(jax.random.fold_in(arg_keys[11], 71), 0)
    neighbours = draw_neighbours(jax.random.fold_in(arg_keys[11], 71), 0)
    wavevectors = jnp.clip(jax.random.uniform(arg_keys[4], (3, K), jnp.float32, -1.0, 1.0) * level_of(arg_keys[4], (3, K), ((1, 2),), -0.4, 0.0), -1.0, 1.0)
    filters = normal_values(arg_keys[5], (K, F), 1.0, 6.0, ((0, 2),), jnp.float32)
    falloffs = jnp.clip(jnp.exp(jax.random.uniform(arg_keys[6], (G,), jnp.float32, math.log(0.05), math.log(2.0))), 0.05, 2.0)
    mixing = normal_values(arg_keys[7], (G, F), 0.15, 2.0, (), jnp.float32)
    norm_gain = jnp.clip(1.0 + 0.1 * jax.random.normal(arg_keys[8], (F,), jnp.float32), 0.5, 1.5)
    in_weight = normal_values(arg_keys[9], (F, H), F ** -0.5, 0.25, ((1, 2),))
    out_weight = normal_values(arg_keys[10], (H, F), H ** -0.5, 0.1875, ((0, 2),))
    return {"features": features, "positions": positions, "occupancy": occupancy, "neighbours": neighbours, "wavevectors": wavevectors, "filters": filters, "falloffs": falloffs, "mixing": mixing, "norm_gain": norm_gain, "in_weight": in_weight, "out_weight": out_weight}


EPS = 1e-06

def wrap_long(along_x, length):
    return jnp.where(along_x > 0.5 * length, along_x - length, jnp.where(along_x < -0.5 * length, along_x + length, along_x))

def phases_of(block_waves, positions):
    return block_waves[0][:, None] * positions[0][None, :] + block_waves[1][:, None] * positions[1][None, :] + block_waves[2][:, None] * positions[2][None, :]

def near_part(masked, positions, neighbours, falloffs, mixing):
    cell_feats = masked.reshape(NCELLS, CAP, F)
    cell_pos = positions.reshape(3, NCELLS, CAP)
    length = jnp.float32(NCELLS)

    def one_cell(cell_index):
        local_pos = cell_pos[:, cell_index]
        summed = jnp.zeros((G, CAP, F), jnp.float32)
        for neighbour in range(NB):
            partner = (cell_index + neighbours[cell_index, neighbour]) % NCELLS
            other_pos = cell_pos[:, partner]
            displace = local_pos[:, :, None] - other_pos[:, None, :]
            along_x = wrap_long(displace[0], length)
            squared = along_x * along_x + displace[1] * displace[1] + displace[2] * displace[2]
            kernel = jnp.exp(-falloffs[:, None, None] * squared[None]).astype(jnp.bfloat16)
            summed = summed + jnp.einsum('gij,jf->gif', kernel.astype(jnp.float32), cell_feats[partner].astype(jnp.float32), precision=lax.Precision.HIGHEST)
        return lax.optimization_barrier(jnp.sum(summed * mixing[:, None, :], axis=0))
    return lax.map(one_cell, jnp.arange(NCELLS, dtype=jnp.int32)).reshape(NCELLS * CAP, F)

def trig_wide(block_waves, positions):
    phases = phases_of(block_waves, positions)
    cosine_block = lax.optimization_barrier(jnp.cos(phases).astype(jnp.bfloat16)).astype(jnp.float32)
    sine_block = lax.optimization_barrier(jnp.sin(phases).astype(jnp.bfloat16)).astype(jnp.float32)
    return (cosine_block, sine_block)

def far_part(masked, positions, wavevectors, filters, count):
    block_rows = math.gcd(K, 512)
    stacked = wavevectors.reshape(3, K // block_rows, block_rows).transpose(1, 0, 2)
    masked_wide = masked.astype(jnp.float32)

    def forward(block_waves):
        cosine_block, sine_block = trig_wide(block_waves, positions)
        return (jnp.dot(cosine_block, masked_wide, precision=lax.Precision.HIGHEST), jnp.dot(sine_block, masked_wide, precision=lax.Precision.HIGHEST))
    cos_factor, sin_factor = lax.map(forward, stacked)
    count_root = jnp.sqrt(count)
    cos_factor = cos_factor.reshape(K, F) / count_root
    sin_factor = sin_factor.reshape(K, F) / count_root
    cos_filtered = (filters * cos_factor).astype(jnp.bfloat16).reshape(K // block_rows, block_rows, F)
    sin_filtered = (filters * sin_factor).astype(jnp.bfloat16).reshape(K // block_rows, block_rows, F)

    def backward(running, pieces):
        block_waves, cos_rows, sin_rows = pieces
        cosine_block, sine_block = trig_wide(block_waves, positions)
        running = running + jnp.dot(cosine_block.T, cos_rows.astype(jnp.float32), precision=lax.Precision.HIGHEST)
        running = running + jnp.dot(sine_block.T, sin_rows.astype(jnp.float32), precision=lax.Precision.HIGHEST)
        return (running, None)
    far_sum, unused = lax.scan(backward, jnp.zeros((NCELLS * CAP, F), jnp.float32), (stacked, cos_filtered, sin_filtered))
    return far_sum / math.sqrt(K)

def reference(features, positions, occupancy, neighbours, wavevectors, filters, falloffs, mixing, norm_gain, in_weight, out_weight):
    slot_place = jnp.arange(NCELLS * CAP, dtype=jnp.int32) % CAP
    is_live = slot_place < jnp.repeat(occupancy, CAP)
    masked = jnp.where(is_live[:, None], features, jnp.zeros_like(features))
    count = jnp.sum(occupancy).astype(jnp.float32)
    near = near_part(masked, positions, neighbours, falloffs, mixing)
    far = far_part(masked, positions, wavevectors, filters, count)
    merged = features.astype(jnp.float32) + near + far
    normed = (merged * lax.rsqrt(lax.optimization_barrier(jnp.mean(merged * merged, axis=-1, keepdims=True)) + EPS) * norm_gain).astype(jnp.bfloat16)
    hidden = jax.nn.silu(jnp.dot(normed, in_weight, preferred_element_type=jnp.float32)).astype(jnp.bfloat16)
    result = merged + jnp.dot(hidden, out_weight, preferred_element_type=jnp.float32)
    return result.astype(jnp.bfloat16)
```

```python
import functools
import math

import jax
import jax.numpy as jnp
from jax import lax
from jax.experimental import pallas as pl
from jax.experimental.pallas import tpu as pltpu
from jax.sharding import PartitionSpec as P

EPS = 1e-06
HW = 2
CHUNKS = 2
TILE = 256

SCALE = 8.0**0.25
SIN_QUARTER = [SCALE * c for c in (1.5707884677838282, -0.6457119641929367, 0.07766728844449011)]
COS_QUARTER = [
    SCALE * c for c in (0.9999999724196053, -1.2336970139164884, 0.2535986397412255, -0.02040833859268099)
]


def horner(x, coefs):
    value = jnp.float32(coefs[-1])
    for coef in coefs[-2::-1]:
        value = value * x + jnp.float32(coef)
    return value


def cos_sin_turns(turns):
    rest = turns - jnp.round(turns)
    square = rest * rest
    sin_quarter = horner(square, SIN_QUARTER) * rest
    cos_quarter = horner(square, COS_QUARTER)
    sin_half = sin_quarter * cos_quarter
    cos_half = jnp.float32(math.sqrt(2.0)) - sin_quarter * sin_quarter
    return jnp.float32(1.0) - sin_half * sin_half, sin_half * cos_half


def forward_body(base, block_rows, reverse, waves_ref, atoms_ref, feats_ref, cos_ref, sin_ref, sum_ref, lhs, rhs, turns):
    rows = lhs.shape[0]
    blocks = feats_ref.shape[0] // TILE
    step = pl.program_id(0)
    sums = [None, None]

    @pl.when(step == 0)
    def _():
        high, middle, low = thirds(atoms_ref[...])
        rhs[...] = jnp.concatenate([high, middle, high, low, high, middle], axis=0).astype(jnp.bfloat16)

    start, first = base
    for part in range(rows // block_rows):
        number = (first + step * (rows // block_rows) + part) ^ reverse[0]
        at = pl.multiple_of(start + number * block_rows, block_rows)
        lhs[part * block_rows : (part + 1) * block_rows, :] = waves_ref[pl.ds(at, block_rows), :]

    def phase(block):
        turns[block % 3] = jnp.dot(
            lhs[...], rhs[:, block * TILE : (block + 1) * TILE], preferred_element_type=jnp.float32
        )

    def fill(block):
        for strip in range(rows // 16):
            at = slice(strip * 16, strip * 16 + 16)
            cos_part, sin_part = cos_sin_turns(turns[block % 3, at, :])
            cos_ref[at, block * TILE : (block + 1) * TILE] = cos_part.astype(jnp.bfloat16)
            sin_ref[at, block * TILE : (block + 1) * TILE] = sin_part.astype(jnp.bfloat16)

    def multiply(block):
        at = slice(block * TILE, (block + 1) * TILE)
        for which, ref in enumerate((cos_ref, sin_ref)):
            term = jnp.dot(ref[:, at], feats_ref[at, :], preferred_element_type=jnp.float32)
            sums[which] = term if sums[which] is None else sums[which] + term

    phase(0)
    for block in range(blocks):
        if block + 1 < blocks:
            phase(block + 1)
        fill(block)
        if block > 0:
            multiply(block - 1)
    multiply(blocks - 1)
    for which in range(2):
        sum_ref[which] = sums[which].astype(sum_ref.dtype)


def forward(reverse, waves, atoms, feats, start, position, count, block_rows, dtype):
    depth = waves.shape[1]
    atom_rows, width = feats.shape
    tile = min(TILE, count)
    trig = jax.ShapeDtypeStruct((count, atom_rows), jnp.bfloat16)
    return pl.pallas_call(
        functools.partial(forward_body, (start, position // block_rows), block_rows),
        grid_spec=pltpu.PrefetchScalarGridSpec(
            num_scalar_prefetch=1,
            grid=(count // tile,),
            in_specs=[
                pl.BlockSpec(waves.shape, lambda k, *_: (0, 0)),
                pl.BlockSpec(atoms.shape, lambda k, *_: (0, 0)),
                pl.BlockSpec(feats.shape, lambda k, *_: (0, 0)),
            ],
            out_specs=[
                pl.BlockSpec((tile, atom_rows), lambda k, *_: (k, 0)),
                pl.BlockSpec((tile, atom_rows), lambda k, *_: (k, 0)),
                pl.BlockSpec((2, tile, width), lambda k, *_: (0, k, 0)),
            ],
            scratch_shapes=[
                pltpu.VMEM((tile, depth), jnp.bfloat16),
                pltpu.VMEM((depth, atom_rows), jnp.bfloat16),
                pltpu.VMEM((3, tile, TILE), jnp.float32),
            ],
        ),
        out_shape=[trig, trig, jax.ShapeDtypeStruct((2, count, width), dtype)],
        cost_estimate=pl.CostEstimate(
            flops=9 * count * atom_rows * width,
            transcendentals=0,
            bytes_accessed=4 * count * atom_rows,
        ),
        name="structure",
    )(reverse, waves, atoms, feats)


def near_body(places, scales, row_ref, left_ref, masked_ref, right_ref, feats_ref, mix_ref, out_ref, wide, kernels, partners):
    cells_per_step = kernels.shape[0]
    cap = wide.shape[1]
    step = pl.program_id(0)
    kinds = mix_ref.shape[0]
    count = places.shape[1]
    halo = left_ref.shape[0]
    inner = masked_ref.shape[0]

    @pl.when(step == 0)
    def _():
        wide[0:halo] = left_ref[...]
        wide[halo : halo + inner] = masked_ref[...]
        wide[halo + inner :] = right_ref[...]

    for part in range(cells_per_step):
        cell = step * cells_per_step + part
        col = jnp.transpose(row_ref[cell + halo])
        for which in range(count):
            place = places[cell, which]
            row = row_ref[place]
            squared = None
            for axis in range(3):
                gap = col[:, axis : axis + 1] - row[axis : axis + 1, :]
                squared = gap * gap if squared is None else squared + gap * gap
            for kind in range(kinds):
                kernels[part, kind * cap : (kind + 1) * cap, which * cap : (which + 1) * cap] = (
                    jnp.exp2(scales[kind] * squared).astype(jnp.bfloat16)
                )
            partners[part, which * cap : (which + 1) * cap, :] = wide[place]
        total = jnp.dot(kernels[part], partners[part], preferred_element_type=jnp.float32)
        at = slice(part * cap, (part + 1) * cap)
        near = feats_ref[at, :].astype(jnp.float32)
        for kind in range(kinds):
            near = near + total[kind * cap : (kind + 1) * cap, :] * mix_ref[kind : kind + 1, :]
        out_ref[at, :] = near


def near_part(places, scales, rows, left, masked, right, feats, mix):
    cells, count = places.shape
    cap, width = masked.shape[1:]
    kinds = mix.shape[0]
    per = 2
    whole3 = lambda a: pl.BlockSpec(a.shape, lambda c, *_: (0, 0, 0))
    return pl.pallas_call(
        near_body,
        grid_spec=pltpu.PrefetchScalarGridSpec(
            num_scalar_prefetch=2,
            grid=(cells // per,),
            in_specs=[
                whole3(rows),
                whole3(left),
                whole3(masked),
                whole3(right),
                pl.BlockSpec((per * cap, width), lambda c, *_: (c, 0)),
                pl.BlockSpec(mix.shape, lambda c, *_: (0, 0)),
            ],
            out_specs=pl.BlockSpec((per * cap, width), lambda c, *_: (c, 0)),
            scratch_shapes=[
                pltpu.VMEM((rows.shape[0], cap, width), jnp.bfloat16),
                pltpu.VMEM((per, kinds * cap, count * cap), jnp.bfloat16),
                pltpu.VMEM((per, count * cap, width), jnp.bfloat16),
            ],
        ),
        out_shape=jax.ShapeDtypeStruct(feats.shape, jnp.float32),
        cost_estimate=pl.CostEstimate(
            flops=8 * cells * cap * cap * count * width * kinds,
            transcendentals=0,
            bytes_accessed=8 * cells * cap * width,
        ),
        name="near",
    )(places, scales, rows, left, masked, right, feats, mix)


def backward_body(pieces, *refs):
    trig = refs[:4]
    filts = refs[4:6]
    acc_ref = refs[6]
    outs = refs[7:]
    contract = (((0,), (0,)), ((), ()))
    total = acc_ref[...]
    for half in range(2):
        for which in range(2):
            total = total + lax.dot_general(
                trig[2 * half + which][...],
                filts[half][which],
                contract,
                preferred_element_type=jnp.float32,
            )
    outs[0][...] = total
    for piece in range(pieces):

        @pl.when(pl.program_id(0) == piece)
        def _(piece=piece):
            outs[1 + piece][...] = total.astype(jnp.bfloat16)


def backward(trig, filts, acc, first, tiles, tile, pieces):
    count = trig[0].shape[0]
    width = acc.shape[1]
    acc_offset = first if acc.shape[0] > tiles * tile else 0
    shapes = [jax.ShapeDtypeStruct((tiles * tile, width), jnp.float32)]
    specs = [pl.BlockSpec((tile, width), lambda i: (i, 0))]
    for _ in range(pieces):
        shapes.append(jax.ShapeDtypeStruct((tile, width), jnp.bfloat16))
        specs.append(pl.BlockSpec((tile, width), lambda i: (0, 0)))
    return pl.pallas_call(
        functools.partial(backward_body, pieces),
        grid=(tiles,),
        in_specs=[pl.BlockSpec((count, tile), lambda i: (0, i + first))] * 4
        + [pl.BlockSpec(filts[0].shape, lambda i: (0, 0, 0))] * 2
        + [pl.BlockSpec((tile, width), lambda i: (i + acc_offset, 0))],
        out_specs=specs,
        out_shape=shapes,
        cost_estimate=pl.CostEstimate(
            flops=16 * count * tiles * tile * width,
            transcendentals=0,
            bytes_accessed=8 * count * tiles * tile + 8 * tiles * tile * width,
        ),
        name="messages",
    )(*trig, *filts, acc)


def mlp_body(side, own_ref, other_ref, gain_ref, in0_ref, in1_ref, out0_ref, out1_ref, result_ref):
    width = own_ref.shape[1]
    mine = side[0]
    own = own_ref[...]
    own_wide = own.astype(jnp.bfloat16).astype(jnp.float32)
    other = other_ref[...].astype(jnp.float32)
    mean = (
        jnp.sum(own_wide * own_wide, axis=1, keepdims=True)
        + jnp.sum(other * other, axis=1, keepdims=True)
    ) / (2 * width)
    scale = lax.rsqrt(mean + EPS)
    normed_own = (own_wide * scale * gain_ref[pl.ds(mine, 1), :]).astype(jnp.bfloat16)
    normed_other = (other * scale * gain_ref[pl.ds(1 - mine, 1), :]).astype(jnp.bfloat16)
    at_own = pl.ds(pl.multiple_of(mine * width, width), width)
    at_other = pl.ds(pl.multiple_of((1 - mine) * width, width), width)
    total = own
    for in_ref, out_ref in ((in0_ref, out0_ref), (in1_ref, out1_ref)):
        value = jnp.dot(normed_own, in_ref[at_own, :], preferred_element_type=jnp.float32)
        value = value + jnp.dot(
            normed_other, in_ref[at_other, :], preferred_element_type=jnp.float32
        )
        half = jnp.float32(0.5) * value
        hidden = (half * jnp.tanh(half) + half).astype(jnp.bfloat16)
        total = total + jnp.dot(hidden, out_ref[...], preferred_element_type=jnp.float32)
    result_ref[...] = total.astype(jnp.bfloat16)


def mlp(side, own, other, piece, gains, weights):
    rows, width = other.shape
    tile = min(256, rows)
    offset = piece * (rows // tile)
    return pl.pallas_call(
        mlp_body,
        grid_spec=pltpu.PrefetchScalarGridSpec(
            num_scalar_prefetch=1,
            grid=(rows // tile,),
            in_specs=[
                pl.BlockSpec((tile, width), lambda i, *_: (i + offset, 0)),
                pl.BlockSpec((tile, width), lambda i, *_: (i, 0)),
                pl.BlockSpec(gains.shape, lambda i, *_: (0, 0)),
            ]
            + [pl.BlockSpec(weight.shape, lambda i, *_: (0, 0)) for weight in weights],
            out_specs=pl.BlockSpec((tile, width), lambda i, *_: (i, 0)),
        ),
        out_shape=jax.ShapeDtypeStruct((rows, width), jnp.bfloat16),
        cost_estimate=pl.CostEstimate(
            flops=2 * rows * width * weights[0].shape[1] * 12,
            transcendentals=0,
            bytes_accessed=8 * rows * width,
        ),
        name="mlp",
    )(side, own, other, gains, *weights)


def thirds(values):
    def rounded(v):
        return v.astype(jnp.bfloat16).astype(jnp.float32)

    high = rounded(values)
    middle = rounded(values - high)
    return high, middle, values - high - middle


def swap(value):
    return lax.ppermute(value, "waves", [(0, 1), (1, 0)])


def across(value, bit):
    count = lax.axis_size("cells")
    return lax.ppermute(value, "cells", [(i, i ^ bit) for i in range(count)])


def shards(
    features,
    positions,
    occupancy,
    neighbours,
    wavevectors,
    filters,
    falloffs,
    mixing,
    norm_gain,
    in_weight,
    out_weight,
):
    devices = lax.axis_size("cells")
    bits = [1 << b for b in range(devices.bit_length() - 1)]
    cell_count = occupancy.shape[0]
    atom_rows, width = features.shape
    capacity = atom_rows // cell_count
    wave_rows = wavevectors.shape[1]
    all_waves = 2 * wave_rows
    chunk_rows = wave_rows // CHUNKS
    block_rows = chunk_rows // devices
    length = jnp.float32(devices * cell_count)
    place = lax.axis_index("cells").astype(jnp.int32)
    side = lax.axis_index("waves").astype(jnp.int32)

    live = (jnp.arange(capacity, dtype=jnp.int32)[None, :] < occupancy[:, None]).reshape(atom_rows, 1)
    masked = jnp.where(live, features, jnp.zeros_like(features))

    reverse = jnp.int32(0)
    for index, bit in enumerate(reversed(bits)):
        reverse = reverse | jnp.where((place & bit) != 0, bits[index], 0).astype(jnp.int32)
    reverse_scalar = reverse.reshape(1)

    def wave_operand(waves):
        padded = jnp.pad(waves * jnp.float32(1.0 / (2.0 * math.pi)), ((0, 5), (0, 0)))
        high = lax.reduce_precision(padded, 8, 7)
        middle = lax.reduce_precision(padded - high, 8, 7)
        low = padded - high - middle
        return jnp.concatenate([high, high, middle, high, low, middle], axis=0).T.astype(jnp.bfloat16)

    atoms = jnp.pad(positions, ((0, 5), (0, 0)))
    other_waves = swap(wavevectors)

    to_right = [(i, (i + 1) % devices) for i in range(devices)]
    to_left = [((i + 1) % devices, i) for i in range(devices)]
    edge = HW * capacity
    left_feats = lax.ppermute(masked[atom_rows - edge :], "cells", to_right)
    right_feats = lax.ppermute(masked[:edge], "cells", to_left)
    left_pos = lax.ppermute(positions[:, atom_rows - edge :], "cells", to_right)
    right_pos = lax.ppermute(positions[:, :edge], "cells", to_left)
    count = jnp.full((8, 128), jnp.sum(occupancy).astype(jnp.float32))
    for bit in bits:
        count = count + across(count, bit)
    count = count[0:1, 0:1]

    def filter_part(chunk, whose):
        return lax.dynamic_slice(
            filters, (chunk * chunk_rows + reverse * block_rows, whose * width), (block_rows, width)
        )

    own_filters = [filter_part(chunk, side) for chunk in range(CHUNKS)]
    sent_filters = jnp.stack([filter_part(chunk, 1 - side) for chunk in range(CHUNKS)])
    other_filters = swap(sent_filters)

    in_other = swap(in_weight)
    hidden_rows = out_weight.shape[0]
    out_own = lax.dynamic_slice(out_weight, (0, side * width), (hidden_rows, width))
    out_other = swap(lax.dynamic_slice(out_weight, (0, (1 - side) * width), (hidden_rows, width)))

    factor = lax.rsqrt(count) * jnp.float32(1.0 / math.sqrt(all_waves))

    trig, totals = [], []
    number = 0
    for waves, rows_of_filter in ((wavevectors, own_filters), (other_waves, other_filters)):
        operand = wave_operand(waves)
        for chunk in range(CHUNKS):
            half = chunk_rows // 2
            cos_far, sin_far, send = forward(
                reverse_scalar, operand, atoms, masked, chunk * chunk_rows, half, half, block_rows, jnp.bfloat16
            )
            cos_near, sin_near, keep = forward(
                reverse_scalar, operand, atoms, masked, chunk * chunk_rows, 0, half, block_rows, jnp.float32
            )
            trig.append((cos_near, sin_near, cos_far, sin_far))
            for index, bit in enumerate(bits):
                summed = keep + across(send, bit).astype(jnp.float32)
                if index + 1 < len(bits):
                    half = summed.shape[1] // 2
                    keep, send = summed[:, :half], summed[:, half:].astype(jnp.bfloat16)
            filt = (summed * rows_of_filter[chunk][None] * factor[None]).astype(jnp.bfloat16)
            for index, bit in enumerate(reversed(bits)):
                came = across(filt, bit)
                if index + 1 < len(bits):
                    filt = jnp.concatenate([filt, came], axis=1)
            totals.append((filt, came))
            number += 1

    shift_left = jnp.where(place == 0, length, 0.0).astype(jnp.float32)
    shift_right = jnp.where(place == devices - 1, length, 0.0).astype(jnp.float32)
    first = jnp.array([[1.0], [0.0], [0.0]], jnp.float32)
    wide_pos = jnp.concatenate(
        [left_pos - first * shift_left, positions, right_pos + first * shift_right], axis=1
    )
    rows = jnp.pad(wide_pos, ((0, 5), (0, 0))).reshape(8, cell_count + 2 * HW, capacity).transpose(1, 0, 2)
    places = jnp.arange(cell_count, dtype=jnp.int32)[:, None] + HW + neighbours
    mix = lax.dynamic_slice(mixing, (0, side * width), (mixing.shape[0], width))
    merged = near_part(
        places,
        falloffs * jnp.float32(-1.0 / math.log(2.0)),
        rows,
        left_feats.reshape(HW, capacity, width),
        masked.reshape(cell_count, capacity, width),
        right_feats.reshape(HW, capacity, width),
        features,
        mix,
    )
    pieces = 4
    tile = atom_rows // pieces
    for number in range(len(trig) - 1):
        (merged,) = backward(trig[number], totals[number], merged, 0, pieces, tile, 0)

    gains = norm_gain.reshape(2, width)
    outs = []
    for call in range(2):
        part, *sends = backward(trig[-1], totals[-1], merged, call * 2, 2, tile, 2)
        for piece in range(2):
            came = swap(sends[piece])
            outs.append(
                mlp(side.reshape(1), part, came, piece, gains, (in_weight, in_other, out_own, out_other))
            )
    return jnp.concatenate(outs, axis=0)


def solution(mesh):
    placed = (
        P("cells", "waves"),
        P(None, "cells"),
        P("cells"),
        P("cells", None),
        P(None, "waves"),
        P("waves", None),
        P(),
        P(),
        P(),
        P(None, "waves"),
        P("waves", None),
    )

    return jax.shard_map(shards, mesh=mesh, in_specs=placed, out_specs=P("cells", "waves"), check_vma=False)
```

```python
import functools
import math

import jax
import jax.numpy as jnp
from jax import lax
from jax.experimental import pallas as pl
from jax.experimental.pallas import tpu as pltpu
from jax.sharding import PartitionSpec as P

EPS = 1e-06
HW = 2
CHUNKS = 2
TILE = 256
FORWARD_ROWS = 128

SCALE = 8.0**0.25
SIN_QUARTER = [SCALE * c for c in (1.5707884677838282, -0.6457119641929367, 0.07766728844449011)]
COS_QUARTER = [
    SCALE * c for c in (0.9999999724196053, -1.2336970139164884, 0.2535986397412255, -0.02040833859268099)
]


def horner(x, coefs):
    value = jnp.float32(coefs[-1])
    for coef in coefs[-2::-1]:
        value = value * x + jnp.float32(coef)
    return value


def cos_sin_turns(turns):
    rest = turns - jnp.round(turns)
    square = rest * rest
    sin_quarter = horner(square, SIN_QUARTER) * rest
    cos_quarter = horner(square, COS_QUARTER)
    sin_half = sin_quarter * cos_quarter
    cos_half = jnp.float32(math.sqrt(2.0)) - sin_quarter * sin_quarter
    return jnp.float32(1.0) - sin_half * sin_half, sin_half * cos_half


def forward_body(
    start, first, block_rows, places, waves_ref, own_pos, other_pos, own_ref, other_ref,
    cos_ref, sin_ref, sum_ref, lhs, rhs, turns,
):
    rows = lhs.shape[0]
    step = pl.program_id(0)
    sums = [None, None]
    atom_rows = own_ref.shape[0]

    @pl.when(step == 0)
    def _():
        for number, ref in enumerate((own_pos, other_pos)):
            high, middle, low = thirds(ref[...])
            rhs[:, number * atom_rows : (number + 1) * atom_rows] = jnp.concatenate(
                [high, middle, high, low, high, middle], axis=0
            ).astype(jnp.bfloat16)

    for part in range(rows // block_rows):
        number = (first + step * (rows // block_rows) + part) ^ places[0]
        at = pl.multiple_of(places[1] + start + number * block_rows, block_rows)
        lhs[part * block_rows : (part + 1) * block_rows, :] = waves_ref[pl.ds(at, block_rows), :]

    blocks = [(ref, base) for ref in (own_ref, other_ref) for base in range(0, atom_rows, TILE)]

    def phase(block):
        turns[block % 3] = jnp.dot(
            lhs[...], rhs[:, block * TILE : (block + 1) * TILE], preferred_element_type=jnp.float32
        )

    def fill(block):
        for strip in range(rows // 16):
            at = slice(strip * 16, strip * 16 + 16)
            cos_part, sin_part = cos_sin_turns(turns[block % 3, at, :])
            cos_ref[at, block * TILE : (block + 1) * TILE] = cos_part.astype(jnp.bfloat16)
            sin_ref[at, block * TILE : (block + 1) * TILE] = sin_part.astype(jnp.bfloat16)

    def multiply(block):
        feats_ref, base = blocks[block]
        feats = feats_ref[base : base + TILE, :]
        at = slice(block * TILE, (block + 1) * TILE)
        for which, ref in enumerate((cos_ref, sin_ref)):
            term = jnp.dot(ref[:, at], feats, preferred_element_type=jnp.float32)
            sums[which] = term if sums[which] is None else sums[which] + term

    phase(0)
    for block in range(len(blocks)):
        if block + 1 < len(blocks):
            phase(block + 1)
        fill(block)
        if block > 0:
            multiply(block - 1)
    multiply(len(blocks) - 1)
    for which in range(2):
        sum_ref[which] = sums[which].astype(sum_ref.dtype)


def forward(places, waves, positions, feats, start, position, count, block_rows, dtype):
    depth = waves.shape[1]
    atom_rows, width = feats[0].shape
    tile = min(FORWARD_ROWS, count)
    trig = jax.ShapeDtypeStruct((count, 2 * atom_rows), jnp.bfloat16)
    return pl.pallas_call(
        functools.partial(forward_body, start, position // block_rows, block_rows),
        grid_spec=pltpu.PrefetchScalarGridSpec(
            num_scalar_prefetch=1,
            grid=(count // tile,),
            in_specs=[
                pl.BlockSpec(array.shape, lambda k, *_: (0, 0))
                for array in (waves, *positions, *feats)
            ],
            out_specs=[
                pl.BlockSpec((tile, 2 * atom_rows), lambda k, *_: (k, 0)),
                pl.BlockSpec((tile, 2 * atom_rows), lambda k, *_: (k, 0)),
                pl.BlockSpec((2, tile, width), lambda k, *_: (0, k, 0)),
            ],
            scratch_shapes=[
                pltpu.VMEM((tile, depth), jnp.bfloat16),
                pltpu.VMEM((depth, 2 * atom_rows), jnp.bfloat16),
                pltpu.VMEM((3, tile, TILE), jnp.float32),
            ],
        ),
        out_shape=[trig, trig, jax.ShapeDtypeStruct((2, count, width), dtype)],
        cost_estimate=pl.CostEstimate(
            flops=18 * count * atom_rows * width,
            transcendentals=0,
            bytes_accessed=8 * count * atom_rows,
        ),
        name="structure",
    )(places, waves, *positions, *feats)


def near_body(base, places, scales, row_ref, left_ref, masked_ref, right_ref, feats_ref, mix_ref, out_ref, wide, kernels, partners):
    cells_per_step = kernels.shape[0]
    cap = wide.shape[1]
    step = pl.program_id(0)
    kinds = mix_ref.shape[0]
    count = places.shape[1]
    halo = left_ref.shape[0]
    inner = masked_ref.shape[0]

    @pl.when(step == 0)
    def _():
        wide[0:halo] = left_ref[...]
        wide[halo : halo + inner] = masked_ref[...]
        wide[halo + inner :] = right_ref[...]

    for part in range(cells_per_step):
        cell = base + step * cells_per_step + part
        col = jnp.transpose(row_ref[cell + halo])
        for which in range(count):
            place = places[cell, which]
            row = row_ref[place]
            squared = None
            for axis in range(3):
                gap = col[:, axis : axis + 1] - row[axis : axis + 1, :]
                squared = gap * gap if squared is None else squared + gap * gap
            for kind in range(kinds):
                kernels[part, kind * cap : (kind + 1) * cap, which * cap : (which + 1) * cap] = (
                    jnp.exp2(scales[kind] * squared).astype(jnp.bfloat16)
                )
            partners[part, which * cap : (which + 1) * cap, :] = wide[place]
        total = jnp.dot(kernels[part], partners[part], preferred_element_type=jnp.float32)
        at = slice(part * cap, (part + 1) * cap)
        near = feats_ref[at, :].astype(jnp.float32)
        for kind in range(kinds):
            near = near + total[kind * cap : (kind + 1) * cap, :] * mix_ref[kind : kind + 1, :]
        out_ref[at, :] = near


def near_part(base, cells, places, scales, rows, left, masked, right, feats, mix):
    count = places.shape[1]
    cap, width = masked.shape[1:]
    kinds = mix.shape[0]
    per = min(8, cells)
    offset = base // per
    whole3 = lambda a: pl.BlockSpec(a.shape, lambda c, *_: (0, 0, 0))
    return pl.pallas_call(
        functools.partial(near_body, base),
        grid_spec=pltpu.PrefetchScalarGridSpec(
            num_scalar_prefetch=2,
            grid=(cells // per,),
            in_specs=[
                whole3(rows),
                whole3(left),
                whole3(masked),
                whole3(right),
                pl.BlockSpec((per * cap, width), lambda c, *_: (c + offset, 0)),
                pl.BlockSpec(mix.shape, lambda c, *_: (0, 0)),
            ],
            out_specs=pl.BlockSpec((per * cap, width), lambda c, *_: (c, 0)),
            scratch_shapes=[
                pltpu.VMEM((rows.shape[0], cap, width), jnp.bfloat16),
                pltpu.VMEM((per, kinds * cap, count * cap), jnp.bfloat16),
                pltpu.VMEM((per, count * cap, width), jnp.bfloat16),
            ],
        ),
        out_shape=jax.ShapeDtypeStruct((cells * cap, width), jnp.float32),
        cost_estimate=pl.CostEstimate(
            flops=8 * cells * cap * cap * count * width * kinds,
            transcendentals=0,
            bytes_accessed=8 * cells * cap * width,
        ),
        name="near",
    )(places, scales, rows, left, masked, right, feats, mix)


def backward_body(has_acc, has_came, *refs):
    trig, filts, rest = refs[:4], refs[4:6], list(refs[6:])
    contract = (((0,), (0,)), ((), ()))
    total = rest.pop(0)[...] if has_acc else None
    if has_came:
        total = total + rest.pop(0)[...].astype(jnp.float32)
    for half in range(2):
        for which in range(2):
            term = lax.dot_general(
                trig[2 * half + which][...],
                filts[half][which],
                contract,
                preferred_element_type=jnp.float32,
            )
            total = term if total is None else total + term
    for ref in rest:
        ref[...] = total.astype(ref.dtype)


def backward(trig, filts, first, count, tile, acc, came, dtypes):
    rows = trig[0].shape[0]
    width = filts[0].shape[2]
    at = first // tile
    args, specs = [], []
    for array in (acc, came):
        if array is not None:
            array, offset = array
            args.append(array)
            specs.append(pl.BlockSpec((tile, width), lambda i, offset=offset: (i + offset, 0)))
    return pl.pallas_call(
        functools.partial(backward_body, acc is not None, came is not None),
        grid=(count // tile,),
        in_specs=[pl.BlockSpec((rows, tile), lambda i: (0, i + at))] * 4
        + [pl.BlockSpec(filts[0].shape, lambda i: (0, 0, 0))] * 2
        + specs,
        out_specs=[pl.BlockSpec((tile, width), lambda i: (i, 0))] * len(dtypes),
        out_shape=[jax.ShapeDtypeStruct((count, width), dtype) for dtype in dtypes],
        cost_estimate=pl.CostEstimate(
            flops=16 * rows * count * width,
            transcendentals=0,
            bytes_accessed=8 * rows * count + 8 * count * width,
        ),
        name="messages",
    )(*trig, *filts, *args)


def mlp_body(side, own_ref, other_ref, gain_ref, in0_ref, in1_ref, out0_ref, out1_ref, *refs):
    result_ref = refs[-1]
    width = own_ref.shape[1]
    mine = side[0]
    own = own_ref[...]
    own_wide = own.astype(jnp.bfloat16).astype(jnp.float32)
    other = other_ref[...].astype(jnp.float32)
    mean = (
        jnp.sum(own_wide * own_wide, axis=1, keepdims=True)
        + jnp.sum(other * other, axis=1, keepdims=True)
    ) / (2 * width)
    scale = lax.rsqrt(mean + EPS)
    normed_own = (own_wide * scale * gain_ref[pl.ds(mine, 1), :]).astype(jnp.bfloat16)
    normed_other = (other * scale * gain_ref[pl.ds(1 - mine, 1), :]).astype(jnp.bfloat16)
    at_own = pl.ds(pl.multiple_of(mine * width, width), width)
    at_other = pl.ds(pl.multiple_of((1 - mine) * width, width), width)
    total = own
    for in_ref, out_ref in ((in0_ref, out0_ref), (in1_ref, out1_ref)):
        value = jnp.dot(normed_own, in_ref[at_own, :], preferred_element_type=jnp.float32)
        value = value + jnp.dot(
            normed_other, in_ref[at_other, :], preferred_element_type=jnp.float32
        )
        half = jnp.float32(0.5) * value
        hidden = (half * jnp.tanh(half) + half).astype(jnp.bfloat16)
        total = total + jnp.dot(hidden, out_ref[...], preferred_element_type=jnp.float32)
    result_ref[...] = total.astype(jnp.bfloat16)


def mlp(side, own, own_at, other, gains, weights, result, first, total_rows):
    rows, width = other.shape
    offset, own_offset = first // rows, own_at // rows
    args = [] if result is None else [result]
    return pl.pallas_call(
        mlp_body,
        grid_spec=pltpu.PrefetchScalarGridSpec(
            num_scalar_prefetch=1,
            grid=(1,),
            in_specs=[
                pl.BlockSpec((rows, width), lambda i, *_: (own_offset, 0)),
                pl.BlockSpec((rows, width), lambda i, *_: (0, 0)),
                pl.BlockSpec(gains.shape, lambda i, *_: (0, 0)),
            ]
            + [pl.BlockSpec(weight.shape, lambda i, *_: (0, 0)) for weight in weights]
            + [pl.BlockSpec(memory_space=pl.ANY)] * len(args),
            out_specs=pl.BlockSpec((rows, width), lambda i, *_: (offset, 0)),
        ),
        out_shape=jax.ShapeDtypeStruct((total_rows, width), jnp.bfloat16),
        input_output_aliases={8: 0} if args else {},
        cost_estimate=pl.CostEstimate(
            flops=2 * rows * width * weights[0].shape[1] * 12,
            transcendentals=0,
            bytes_accessed=8 * rows * width,
        ),
        name="mlp",
    )(side, own, other, gains, *weights, *args)


def thirds(values):
    def rounded(v):
        return v.astype(jnp.bfloat16).astype(jnp.float32)

    high = rounded(values)
    middle = rounded(values - high)
    return high, middle, values - high - middle


def swap(value):
    return lax.ppermute(value, "waves", [(0, 1), (1, 0)])


def across(value, bit):
    count = lax.axis_size("cells")
    return lax.ppermute(value, "cells", [(i, i ^ bit) for i in range(count)])


def shards(
    features,
    positions,
    occupancy,
    neighbours,
    wavevectors,
    filters,
    falloffs,
    mixing,
    norm_gain,
    in_weight,
    out_weight,
):
    devices = lax.axis_size("cells")
    bits = [1 << b for b in range(devices.bit_length() - 1)]
    core_bit, ring_bits = bits[0], bits[1:]
    group = devices // 2
    cell_count = occupancy.shape[0]
    atom_rows, width = features.shape
    capacity = atom_rows // cell_count
    wave_rows = wavevectors.shape[1]
    all_waves = 2 * wave_rows
    own_waves = wave_rows // 2
    chunk_rows = own_waves // CHUNKS
    block_rows = chunk_rows // group
    length = jnp.float32(devices * cell_count)
    place = lax.axis_index("cells").astype(jnp.int32)
    side = lax.axis_index("waves").astype(jnp.int32)
    core = place & core_bit

    live = (jnp.arange(capacity, dtype=jnp.int32)[None, :] < occupancy[:, None]).reshape(atom_rows, 1)
    masked = jnp.where(live, features, jnp.zeros_like(features))
    atoms = jnp.pad(positions, ((0, 5), (0, 0)))

    pair_feats = (masked, across(masked, core_bit))
    pair_atoms = (atoms, across(atoms, core_bit))

    reverse = jnp.int32(0)
    for index, bit in enumerate(reversed(ring_bits)):
        reverse = reverse | jnp.where((place & bit) != 0, 1 << index, 0).astype(jnp.int32)
    places_of_waves = jnp.stack([reverse, core * own_waves])

    def wave_operand(waves):
        padded = jnp.pad(waves * jnp.float32(1.0 / (2.0 * math.pi)), ((0, 5), (0, 0)))
        high = lax.reduce_precision(padded, 8, 7)
        middle = lax.reduce_precision(padded - high, 8, 7)
        low = padded - high - middle
        return jnp.concatenate([high, high, middle, high, low, middle], axis=0).T.astype(jnp.bfloat16)

    other_waves = swap(wavevectors)

    to_right = [(i, (i + 1) % devices) for i in range(devices)]
    to_left = [((i + 1) % devices, i) for i in range(devices)]
    edge = HW * capacity
    left_feats = lax.ppermute(masked[atom_rows - edge :], "cells", to_right)
    right_feats = lax.ppermute(masked[:edge], "cells", to_left)
    left_pos = lax.ppermute(positions[:, atom_rows - edge :], "cells", to_right)
    right_pos = lax.ppermute(positions[:, :edge], "cells", to_left)
    count = jnp.full((8, 128), jnp.sum(occupancy).astype(jnp.float32))
    for bit in bits:
        count = count + across(count, bit)
    count = count[0:1, 0:1]

    def filter_part(chunk, whose):
        row = core * own_waves + chunk * chunk_rows + reverse * block_rows
        return lax.dynamic_slice(filters, (row, whose * width), (block_rows, width))

    own_filters = [filter_part(chunk, side) for chunk in range(CHUNKS)]
    sent_filters = jnp.stack([filter_part(chunk, 1 - side) for chunk in range(CHUNKS)])
    other_filters = swap(sent_filters)

    in_other = swap(in_weight)
    hidden_rows = out_weight.shape[0]
    out_own = lax.dynamic_slice(out_weight, (0, side * width), (hidden_rows, width))
    out_other = swap(lax.dynamic_slice(out_weight, (0, (1 - side) * width), (hidden_rows, width)))

    factor = lax.rsqrt(count) * jnp.float32(1.0 / math.sqrt(all_waves))

    trig, totals = [], []
    number = 0
    for waves, rows_of_filter in ((wavevectors, own_filters), (other_waves, other_filters)):
        operand = wave_operand(waves)
        for chunk in range(CHUNKS):
            half = chunk_rows // 2
            cos_far, sin_far, send = forward(
                places_of_waves, operand, pair_atoms, pair_feats, chunk * chunk_rows, half, half, block_rows, jnp.bfloat16
            )
            cos_near, sin_near, keep = forward(
                places_of_waves, operand, pair_atoms, pair_feats, chunk * chunk_rows, 0, half, block_rows, jnp.float32
            )
            trig.append((cos_near, sin_near, cos_far, sin_far))
            for index, bit in enumerate(ring_bits):
                summed = keep + across(send, bit).astype(jnp.float32)
                if index + 1 < len(ring_bits):
                    half = summed.shape[1] // 2
                    keep, send = summed[:, :half], summed[:, half:].astype(jnp.bfloat16)
            filt = (summed * rows_of_filter[chunk][None] * factor[None]).astype(jnp.bfloat16)
            for index, bit in enumerate(reversed(ring_bits)):
                came = across(filt, bit)
                if index + 1 < len(ring_bits):
                    filt = jnp.concatenate([filt, came], axis=1)
            totals.append((filt, came))
            number += 1

    shift_left = jnp.where(place == 0, length, 0.0).astype(jnp.float32)
    shift_right = jnp.where(place == devices - 1, length, 0.0).astype(jnp.float32)
    first = jnp.array([[1.0], [0.0], [0.0]], jnp.float32)
    wide_pos = jnp.concatenate(
        [left_pos - first * shift_left, positions, right_pos + first * shift_right], axis=1
    )
    rows = jnp.pad(wide_pos, ((0, 5), (0, 0))).reshape(8, cell_count + 2 * HW, capacity).transpose(1, 0, 2)
    places = jnp.arange(cell_count, dtype=jnp.int32)[:, None] + HW + neighbours
    mix = lax.dynamic_slice(mixing, (0, side * width), (mixing.shape[0], width))
    half_cells = cell_count // 2
    half_rows = atom_rows // 2
    own = []
    for half in range(2):
        own.append(
            near_part(
                half * half_cells,
                half_cells,
                places,
                falloffs * jnp.float32(-1.0 / math.log(2.0)),
                rows,
                left_feats.reshape(HW, capacity, width),
                masked.reshape(cell_count, capacity, width),
                right_feats.reshape(HW, capacity, width),
                features,
                mix,
            )
        )

    f32, bf16 = jnp.float32, jnp.bfloat16
    other = None
    tile = half_rows
    mine = None
    for number in range(len(trig) - 1):
        (other,) = backward(
            trig[number], totals[number], atom_rows, atom_rows, tile,
            None if other is None else (other, 0), None, (f32,),
        )
        if mine is None:
            mine = [
                backward(
                    trig[number], totals[number], half * half_rows, half_rows, half_rows,
                    (own[half], 0), None, (f32,),
                )[0]
                for half in range(2)
            ]
            mine = [(mine[0], 0), (mine[1], 0)]
        else:
            mine = [
                (
                    backward(
                        trig[number], totals[number], half * half_rows, half_rows, half_rows,
                        mine[half], None, (f32,),
                    )[0],
                    0,
                )
                for half in range(2)
            ]
    came = []
    for half in range(2):
        (send,) = backward(
            trig[-1], totals[-1], atom_rows + half * half_rows, half_rows, half_rows,
            (other, half), None, (bf16,),
        )
        came.append(across(send, core_bit))
    gains = norm_gain.reshape(2, width)
    weights = (in_weight, in_other, out_own, out_other)
    result = None
    for half in range(2):
        part, send = backward(
            trig[-1], totals[-1], half * half_rows, half_rows, half_rows,
            mine[half], (came[half], 0), (f32, bf16),
        )
        pieces = 1 if half == 0 else 2
        piece_rows = half_rows // pieces
        for piece in range(pieces):
            arrived = swap(send[piece * piece_rows : (piece + 1) * piece_rows])
            result = mlp(
                side.reshape(1), part, piece * piece_rows, arrived, gains, weights, result,
                half * half_rows + piece * piece_rows, atom_rows,
            )
    return result


def solution(mesh):
    placed = (
        P("cells", "waves"),
        P(None, "cells"),
        P("cells"),
        P("cells", None),
        P(None, "waves"),
        P("waves", None),
        P(),
        P(),
        P(),
        P(None, "waves"),
        P("waves", None),
    )

    return jax.shard_map(
        shards, mesh=mesh, in_specs=placed, out_specs=P("cells", "waves"), check_vma=False
    )
```

```python
import functools
import math

import jax
import jax.numpy as jnp
from jax import lax
from jax.experimental import pallas as pl
from jax.experimental.pallas import tpu as pltpu
from jax.sharding import PartitionSpec as P

EPS = 1e-06
HW = 2
SHARES = ((1.0,), (1.0,))
GROUPS = (1,)
TILE = 256
FORWARD_ROWS = 256

SIN_1, SIN_0, SIN_BY = -8.313817368817206, 20.224572228345814, 12.875426983082301
COS_ROOT, COS_1, COS_0 = 0.9993568028372194, -11.426868481113639, 49.031109066681445
COS_BY = -48.99957374784235
HALF = SIN_BY**2 / 2.0
WHOLE_COS = (SIN_BY * COS_BY) ** 2 / 8.0
WHOLE_SIN = SIN_BY**3 * COS_BY / 8.0


def cos_sin_turns(turns):
    f32 = jnp.float32
    rest = turns - jnp.round(turns)
    square = rest * rest
    sin_quarter = rest * ((square + f32(SIN_1)) * square + f32(SIN_0))
    cos_quarter = (square - f32(COS_ROOT)) * ((square + f32(COS_1)) * square + f32(COS_0))
    sin_half = sin_quarter * cos_quarter
    cos_half = f32(HALF) - sin_quarter * sin_quarter
    return f32(WHOLE_COS) - sin_half * sin_half, sin_half * cos_half


def forward_body(
    start, first, block_rows, places, waves_ref, own_pos, other_pos, own_ref, other_ref,
    cos_ref, sin_ref, sum_ref, turned, lhs, rhs, turns,
):
    rows = lhs.shape[0]
    step = pl.program_id(0)
    sums = [None, None]
    atom_rows = own_ref.shape[0]

    @pl.when(step == 0)
    def _():
        for number, ref in enumerate((own_pos, other_pos)):
            keep = lax.broadcasted_iota(jnp.int32, ref.shape, 0) < 3
            high, middle, low = thirds(jnp.where(keep, ref[...], jnp.float32(0)))
            rhs[:, number * atom_rows : (number + 1) * atom_rows] = jnp.concatenate(
                [high, middle, high, low, high, middle], axis=0
            ).astype(jnp.bfloat16)

    for part in range(rows // block_rows):
        number = (first + step * (rows // block_rows) + part) ^ places[0]
        at = pl.multiple_of(places[1] + start + number * block_rows, block_rows)
        turned[part * block_rows : (part + 1) * block_rows, :] = waves_ref[pl.ds(at, block_rows), :]
    high, middle, low = thirds(turned[...])
    lhs[...] = jnp.concatenate([high, high, middle, high, low, middle], axis=1).astype(jnp.bfloat16)

    blocks = [(ref, base) for ref in (own_ref, other_ref) for base in range(0, atom_rows, TILE)]

    def phase(block):
        turns[block % 3] = jnp.dot(
            lhs[...], rhs[:, block * TILE : (block + 1) * TILE], preferred_element_type=jnp.float32
        )

    def fill(block):
        for strip in range(rows // 16):
            at = slice(strip * 16, strip * 16 + 16)
            cos_part, sin_part = cos_sin_turns(turns[block % 3, at, :])
            cos_ref[at, block * TILE : (block + 1) * TILE] = cos_part.astype(jnp.bfloat16)
            sin_ref[at, block * TILE : (block + 1) * TILE] = sin_part.astype(jnp.bfloat16)

    def multiply(block):
        feats_ref, base = blocks[block]
        feats = feats_ref[base : base + TILE, :]
        at = slice(block * TILE, (block + 1) * TILE)
        for which, ref in enumerate((cos_ref, sin_ref)):
            term = jnp.dot(ref[:, at], feats, preferred_element_type=jnp.float32)
            sums[which] = term if sums[which] is None else sums[which] + term

    phase(0)
    for block in range(len(blocks)):
        if block + 1 < len(blocks):
            phase(block + 1)
        fill(block)
        if block > 0:
            multiply(block - 1)
    multiply(len(blocks) - 1)
    for which in range(2):
        sum_ref[which] = sums[which].astype(sum_ref.dtype)


def forward(places, waves, positions, feats, start, position, count, block_rows, dtype):
    depth = waves.shape[1]
    atom_rows, width = feats[0].shape
    tile = min(FORWARD_ROWS, count)
    trig = jax.ShapeDtypeStruct((count, 2 * atom_rows), jnp.bfloat16)
    return pl.pallas_call(
        functools.partial(forward_body, start, position // block_rows, block_rows),
        grid_spec=pltpu.PrefetchScalarGridSpec(
            num_scalar_prefetch=1,
            grid=(count // tile,),
            in_specs=[
                pl.BlockSpec(array.shape, lambda k, *_: (0, 0))
                for array in (waves, *positions, *feats)
            ],
            out_specs=[
                pl.BlockSpec((tile, 2 * atom_rows), lambda k, *_: (k, 0)),
                pl.BlockSpec((tile, 2 * atom_rows), lambda k, *_: (k, 0)),
                pl.BlockSpec((2, tile, width), lambda k, *_: (0, k, 0)),
            ],
            scratch_shapes=[
                pltpu.VMEM((tile, depth), jnp.float32),
                pltpu.VMEM((tile, 6 * depth), jnp.bfloat16),
                pltpu.VMEM((6 * depth, 2 * atom_rows), jnp.bfloat16),
                pltpu.VMEM((3, tile, TILE), jnp.float32),
            ],
        ),
        out_shape=[trig, trig, jax.ShapeDtypeStruct((2, count, width), dtype)],
        cost_estimate=pl.CostEstimate(
            flops=18 * count * atom_rows * width,
            transcendentals=0,
            bytes_accessed=8 * count * atom_rows,
        ),
        name="structure",
    )(places, waves, *positions, *feats)


def near_body(base, places, scales, row_ref, left_ref, masked_ref, right_ref, feats_ref, mix_ref, *refs):
    out_ref, wide, kernels, partners = refs[-4:]
    cells_per_step = kernels.shape[0]
    cap = wide.shape[1]
    step = pl.program_id(0)
    kinds = mix_ref.shape[0]
    count = places.shape[1]
    halo = left_ref.shape[0]
    inner = masked_ref.shape[0]

    @pl.when(step == 0)
    def _():
        wide[0:halo] = left_ref[...]
        wide[halo : halo + inner] = masked_ref[...]
        wide[halo + inner :] = right_ref[...]

    for part in range(cells_per_step):
        cell = base + step * cells_per_step + part
        col = jnp.transpose(row_ref[cell + halo])
        for which in range(count):
            place = places[cell, which]
            row = row_ref[place]
            squared = None
            for axis in range(3):
                gap = col[:, axis : axis + 1] - row[axis : axis + 1, :]
                squared = gap * gap if squared is None else squared + gap * gap
            for kind in range(kinds):
                kernels[part, kind * cap : (kind + 1) * cap, which * cap : (which + 1) * cap] = (
                    jnp.exp2(scales[kind] * squared).astype(jnp.bfloat16)
                )
            partners[part, which * cap : (which + 1) * cap, :] = wide[place]
        total = jnp.dot(kernels[part], partners[part], preferred_element_type=jnp.float32)
        at = slice(part * cap, (part + 1) * cap)
        near = feats_ref[at, :].astype(jnp.float32)
        for kind in range(kinds):
            near = near + total[kind * cap : (kind + 1) * cap, :] * mix_ref[kind : kind + 1, :]
        out_ref[at, :] = near


def near_part(base, cells, places, scales, rows, left, masked, right, feats, mix, result):
    count = places.shape[1]
    cap, width = masked.shape[1:]
    kinds = mix.shape[0]
    per = min(4, cells)
    offset = base // per
    args = [] if result is None else [result]
    whole3 = lambda a: pl.BlockSpec(a.shape, lambda c, *_: (0, 0, 0))
    return pl.pallas_call(
        functools.partial(near_body, base),
        grid_spec=pltpu.PrefetchScalarGridSpec(
            num_scalar_prefetch=2,
            grid=(cells // per,),
            in_specs=[
                whole3(rows),
                whole3(left),
                whole3(masked),
                whole3(right),
                pl.BlockSpec((per * cap, width), lambda c, *_: (c + offset, 0)),
                pl.BlockSpec(mix.shape, lambda c, *_: (0, 0)),
            ]
            + [pl.BlockSpec(memory_space=pl.ANY)] * len(args),
            out_specs=pl.BlockSpec((per * cap, width), lambda c, *_: (c + offset, 0)),
            scratch_shapes=[
                pltpu.VMEM((rows.shape[0], cap, width), jnp.bfloat16),
                pltpu.VMEM((per, kinds * cap, count * cap), jnp.bfloat16),
                pltpu.VMEM((per, count * cap, width), jnp.bfloat16),
            ],
        ),
        out_shape=jax.ShapeDtypeStruct(feats.shape, jnp.float32),
        input_output_aliases={8: 0} if args else {},
        cost_estimate=pl.CostEstimate(
            flops=8 * cells * cap * cap * count * width * kinds,
            transcendentals=0,
            bytes_accessed=8 * cells * cap * width,
        ),
        name="near",
    )(places, scales, rows, left, masked, right, feats, mix, *args)


def backward_body(parts, has_acc, has_came, *refs):
    refs = list(refs)
    trig, filts, rest = refs[: 2 * parts], refs[2 * parts : 3 * parts], refs[3 * parts :]
    contract = (((0,), (0,)), ((), ()))
    total = rest.pop(0)[...] if has_acc else None
    if has_came:
        total = total + rest.pop(0)[...].astype(jnp.float32)
    for part in range(parts):
        for which in range(2):
            term = lax.dot_general(
                trig[2 * part + which][...],
                filts[part][which],
                contract,
                preferred_element_type=jnp.float32,
            )
            total = term if total is None else total + term
    for ref in rest:
        ref[...] = total.astype(ref.dtype)


def backward(chunks, first, count, tile, acc, came, dtypes):
    parts = [part for chunk in chunks for part in chunk]
    width = parts[0][2].shape[2]
    at = first // tile
    args, specs = [], []
    for array in (acc, came):
        if array is not None:
            array, offset = array
            args.append(array)
            specs.append(pl.BlockSpec((tile, width), lambda i, offset=offset // tile: (i + offset, 0)))
    trig = [array for cos, sin, _ in parts for array in (cos, sin)]
    filts = [filt for _, _, filt in parts]
    rows = sum(cos.shape[0] for cos, _, _ in parts)
    return pl.pallas_call(
        functools.partial(backward_body, len(parts), acc is not None, came is not None),
        grid=(count // tile,),
        in_specs=[pl.BlockSpec((array.shape[0], tile), lambda i: (0, i + at)) for array in trig]
        + [pl.BlockSpec(filt.shape, lambda i: (0, 0, 0)) for filt in filts]
        + specs,
        out_specs=[pl.BlockSpec((tile, width), lambda i: (i, 0))] * len(dtypes),
        out_shape=[jax.ShapeDtypeStruct((count, width), dtype) for dtype in dtypes],
        cost_estimate=pl.CostEstimate(
            flops=8 * rows * count * width,
            transcendentals=0,
            bytes_accessed=4 * rows * count + 8 * count * width,
        ),
        name="messages",
    )(*trig, *filts, *args)


def mlp_body(side, own_ref, other_ref, gain_ref, in_ref, out_ref, both_ref, *refs):
    result_ref = refs[-1]
    width = own_ref.shape[1]
    hidden_count = in_ref.shape[1]
    mine = side[0]
    own = own_ref[...]
    own_wide = own.astype(jnp.bfloat16).astype(jnp.float32)
    other = other_ref[...].astype(jnp.float32)
    mean = (
        jnp.sum(own_wide * own_wide, axis=1, keepdims=True)
        + jnp.sum(other * other, axis=1, keepdims=True)
    ) / (2 * width)
    scale = lax.rsqrt(mean + EPS)
    normed_own = (own_wide * scale * gain_ref[pl.ds(mine, 1), :]).astype(jnp.bfloat16)
    normed_other = (other * scale * gain_ref[pl.ds(1 - mine, 1), :]).astype(jnp.bfloat16)
    at_own = pl.ds(pl.multiple_of(mine * width, width), width)
    at_other = pl.ds(pl.multiple_of((1 - mine) * width, width), width)
    total = own
    hidden_columns = slice(0, hidden_count)
    halves = (
        (in_ref.at[:, :], out_ref.at[:, :]),
        (both_ref.at[:, hidden_columns], both_ref.at[:, hidden_count:]),
    )
    for in_half, out_half in halves:
        value = jnp.dot(normed_own, in_half[at_own, :], preferred_element_type=jnp.float32)
        value = value + jnp.dot(
            normed_other, in_half[at_other, :], preferred_element_type=jnp.float32
        )
        half = jnp.float32(0.5) * value
        hidden = (half * jnp.tanh(half) + half).astype(jnp.bfloat16)
        total = total + jnp.dot(hidden, out_half[...], preferred_element_type=jnp.float32)
    result_ref[...] = total.astype(jnp.bfloat16)


def mlp(side, own, own_at, other, gains, weights, result, first, total_rows):
    rows, width = other.shape
    offset, own_offset = first // rows, own_at // rows
    args = [] if result is None else [result]
    return pl.pallas_call(
        mlp_body,
        grid_spec=pltpu.PrefetchScalarGridSpec(
            num_scalar_prefetch=1,
            grid=(1,),
            in_specs=[
                pl.BlockSpec((rows, width), lambda i, *_: (own_offset, 0)),
                pl.BlockSpec((rows, width), lambda i, *_: (0, 0)),
                pl.BlockSpec(gains.shape, lambda i, *_: (0, 0)),
            ]
            + [pl.BlockSpec(weight.shape, lambda i, *_: (0, 0)) for weight in weights]
            + [pl.BlockSpec(memory_space=pl.ANY)] * len(args),
            out_specs=pl.BlockSpec((rows, width), lambda i, *_: (offset, 0)),
        ),
        out_shape=jax.ShapeDtypeStruct((total_rows, width), jnp.bfloat16),
        input_output_aliases={7: 0} if args else {},
        cost_estimate=pl.CostEstimate(
            flops=2 * rows * width * weights[0].shape[1] * 12,
            transcendentals=0,
            bytes_accessed=8 * rows * width,
        ),
        name="mlp",
    )(side, own, other, gains, *weights, *args)


def thirds(values):
    def rounded(v):
        return v.astype(jnp.bfloat16).astype(jnp.float32)

    high = rounded(values)
    middle = rounded(values - high)
    return high, middle, values - high - middle


def swap(value):
    return lax.ppermute(value, "waves", [(0, 1), (1, 0)])


def across(value, bit):
    count = lax.axis_size("cells")
    return lax.ppermute(value, "cells", [(i, i ^ bit) for i in range(count)])


def shards(
    features,
    positions,
    occupancy,
    neighbours,
    wavevectors,
    filters,
    falloffs,
    mixing,
    norm_gain,
    in_weight,
    out_weight,
):
    devices = lax.axis_size("cells")
    bits = [1 << b for b in range(devices.bit_length() - 1)]
    core_bit, ring_bits = bits[0], bits[1:]
    group = devices // 2
    cell_count = occupancy.shape[0]
    atom_rows, width = features.shape
    capacity = atom_rows // cell_count
    wave_rows = wavevectors.shape[1]
    all_waves = 2 * wave_rows
    own_waves = wave_rows // 2
    length = jnp.float32(devices * cell_count)
    place = lax.axis_index("cells").astype(jnp.int32)
    side = lax.axis_index("waves").astype(jnp.int32)
    core = place & core_bit

    live = jnp.arange(capacity, dtype=jnp.int32)[None, :, None] < occupancy[:, None, None]
    masked = jnp.where(live, features.reshape(cell_count, capacity, width), jnp.bfloat16(0)).reshape(
        atom_rows, width
    )
    filled = jnp.pad(occupancy.astype(jnp.float32)[None, :], ((0, 4), (0, atom_rows - cell_count)))
    atoms = jnp.concatenate([positions, filled], axis=0)

    pair_feats = (masked, across(masked, core_bit))
    pair_atoms = (atoms, across(atoms, core_bit))

    reverse = jnp.int32(0)
    for index, bit in enumerate(reversed(ring_bits)):
        reverse = reverse | jnp.where((place & bit) != 0, 1 << index, 0).astype(jnp.int32)
    places_of_waves = jnp.stack([reverse, core * own_waves])

    def wave_operand(waves):
        return jnp.pad(waves * jnp.float32(1.0 / (2.0 * math.pi)), ((0, 5), (0, 0))).T

    other_waves = swap(wavevectors)

    to_right = [(i, (i + 1) % devices) for i in range(devices)]
    to_left = [((i + 1) % devices, i) for i in range(devices)]
    edge = HW * capacity
    left_feats = lax.ppermute(masked[atom_rows - edge :], "cells", to_right)
    right_feats = lax.ppermute(masked[:edge], "cells", to_left)
    left_pos = lax.ppermute(positions[:, atom_rows - edge :], "cells", to_right)
    right_pos = lax.ppermute(positions[:, :edge], "cells", to_left)
    count = jnp.sum(filled[0, :cell_count] + pair_atoms[1][3, :cell_count])
    count = jnp.full((8, 128), count)
    for bit in ring_bits:
        count = count + across(count, bit)
    count = count[0:1, 0:1]

    def filter_part(start, rows, whose):
        row = core * own_waves + start + reverse * (rows // group)
        return lax.dynamic_slice(filters, (row, whose * width), (rows // group, width))

    unit = 32 * group
    splits = []
    for shares in SHARES:
        begin, pieces_of_half = 0, []
        for share in shares:
            rows_of = max(unit, int(own_waves * share) // unit * unit)
            rows_of = min(rows_of, own_waves - begin)
            if rows_of > 0:
                pieces_of_half.append((begin, rows_of))
            begin += rows_of
        splits.append(pieces_of_half)
    own_filters = [filter_part(start, rows, side) for start, rows in splits[0]]
    sent_filters = jnp.concatenate(
        [filter_part(start, rows, 1 - side) for start, rows in splits[1]], axis=0
    )
    came_filters = swap(sent_filters)
    other_filters = [
        came_filters[start // group : (start + rows) // group] for start, rows in splits[1]
    ]

    hidden_rows = out_weight.shape[0]
    out_own = lax.dynamic_slice(out_weight, (0, side * width), (hidden_rows, width))
    out_sent = lax.dynamic_slice(out_weight, (0, (1 - side) * width), (hidden_rows, width))
    both = swap(jnp.concatenate([in_weight, out_sent], axis=1))

    factor = lax.rsqrt(count) * jnp.float32(1.0 / math.sqrt(all_waves))
    factors = jnp.stack(
        [factor * jnp.float32(WHOLE_COS**-2), factor * jnp.float32(WHOLE_SIN**-2)]
    )

    chunks = []
    for waves, pieces_of_half, filter_rows in (
        (wavevectors, splits[0], own_filters),
        (other_waves, splits[1], other_filters),
    ):
        operand = wave_operand(waves)
        for (start, rows_of), rows_of_filter in zip(pieces_of_half, filter_rows):
            number = len(chunks)
            scaled = lax.optimization_barrier(rows_of_filter[None] * factors)
            half = rows_of // 2
            cos_far, sin_far, send = forward(
                places_of_waves, operand, pair_atoms, pair_feats, start, half, half, rows_of // group, jnp.bfloat16
            )
            cos_near, sin_near, keep = forward(
                places_of_waves, operand, pair_atoms, pair_feats, start, 0, half, rows_of // group, jnp.float32
            )
            for index, bit in enumerate(ring_bits):
                summed = keep + across(send, bit).astype(jnp.float32)
                if index + 1 < len(ring_bits):
                    half = summed.shape[1] // 2
                    keep, send = summed[:, :half], summed[:, half:].astype(jnp.bfloat16)
            filt = (summed * scaled).astype(jnp.bfloat16)
            for index, bit in enumerate(reversed(ring_bits)):
                came = across(filt, bit)
                if index + 1 < len(ring_bits):
                    filt = jnp.concatenate([filt, came], axis=1)
            chunks.append([(cos_near, sin_near, filt), (cos_far, sin_far, came)])

    shift_left = jnp.where(place == 0, length, 0.0).astype(jnp.float32)
    shift_right = jnp.where(place == devices - 1, length, 0.0).astype(jnp.float32)
    first = jnp.array([[1.0], [0.0], [0.0]], jnp.float32)
    wide_pos = jnp.concatenate(
        [left_pos - first * shift_left, positions, right_pos + first * shift_right], axis=1
    )
    rows = jnp.pad(wide_pos, ((0, 5), (0, 0))).reshape(8, cell_count + 2 * HW, capacity).transpose(1, 0, 2)
    places = jnp.arange(cell_count, dtype=jnp.int32)[:, None] + HW + neighbours
    mix = lax.dynamic_slice(mixing, (0, side * width), (mixing.shape[0], width))
    half_cells = cell_count // 2
    half_rows = atom_rows // 2
    mine = None
    for half in range(2):
        mine = near_part(
            half * half_cells,
            half_cells,
            places,
            falloffs * jnp.float32(-1.0 / math.log(2.0)),
            rows,
            left_feats.reshape(HW, capacity, width),
            masked.reshape(cell_count, capacity, width),
            right_feats.reshape(HW, capacity, width),
            features,
            mix,
            mine,
        )

    f32, bf16 = jnp.float32, jnp.bfloat16
    other = None
    at = 0
    for number, size in enumerate(GROUPS):
        taken = chunks[at : at + size] if number + 1 < len(GROUPS) else chunks[at:-1]
        at += size
        if not taken:
            continue
        (other,) = backward(
            taken, atom_rows, atom_rows, half_rows, None if other is None else (other, 0), None, (f32,)
        )
        (mine,) = backward(taken, 0, atom_rows, half_rows, (mine, 0), None, (f32,))
    last = chunks[-1:]
    came = []
    for half in range(2):
        (send,) = backward(
            last, atom_rows + half * half_rows, half_rows, half_rows // 2, (other, half * half_rows), None, (bf16,)
        )
        came.append(across(send, core_bit))
    gains = norm_gain.reshape(2, width)
    weights = (in_weight, out_own, both)
    result = None
    for half in range(2):
        part, send = backward(
            last, half * half_rows, half_rows, half_rows // 2, (mine, half * half_rows), (came[half], 0), (f32, bf16)
        )
        pieces = 1 if half == 0 else 2
        piece_rows = half_rows // pieces
        for piece in range(pieces):
            arrived = swap(send[piece * piece_rows : (piece + 1) * piece_rows])
            result = mlp(
                side.reshape(1), part, piece * piece_rows, arrived, gains, weights, result,
                half * half_rows + piece * piece_rows, atom_rows,
            )
    return result


def solution(mesh):
    placed = (
        P("cells", "waves"),
        P(None, "cells"),
        P("cells"),
        P("cells", None),
        P(None, "waves"),
        P("waves", None),
        P(),
        P(),
        P(),
        P(None, "waves"),
        P("waves", None),
    )

    return jax.shard_map(
        shards, mesh=mesh, in_specs=placed, out_specs=P("cells", "waves"), check_vma=False
    )
```

```python
import functools
import math

import jax
import jax.numpy as jnp
from jax import lax
from jax.experimental import pallas as pl
from jax.experimental.pallas import tpu as pltpu
from jax.sharding import PartitionSpec as P

EPS = 1e-06
HW = 2
SHARES = ((1.0,), (1.0,))
GROUPS = (1,)
TILE = 256
FORWARD_ROWS = 256
LIMIT = pltpu.CompilerParams(vmem_limit_bytes=16 << 20)

SIN_1, SIN_0, SIN_BY = -8.313817368817206, 20.224572228345814, 12.875426983082301
COS_ROOT, COS_1, COS_0 = 0.9993568028372194, -11.426868481113639, 49.031109066681445
COS_BY = -48.99957374784235
HALF = SIN_BY**2 / 2.0
WHOLE_COS = (SIN_BY * COS_BY) ** 2 / 8.0
WHOLE_SIN = SIN_BY**3 * COS_BY / 8.0


def cos_sin_turns(turns):
    f32 = jnp.float32
    rest = turns - jnp.round(turns)
    square = rest * rest
    sin_quarter = rest * ((square + f32(SIN_1)) * square + f32(SIN_0))
    cos_quarter = (square - f32(COS_ROOT)) * ((square + f32(COS_1)) * square + f32(COS_0))
    sin_half = sin_quarter * cos_quarter
    cos_half = f32(HALF) - sin_quarter * sin_quarter
    return f32(WHOLE_COS) - sin_half * sin_half, sin_half * cos_half


def forward_body(
    start, first, block_rows, places, waves_ref, own_pos, other_pos, own_ref, other_ref,
    cos_ref, sin_ref, sum_ref, columns, turned, lhs, rhs, turns,
):
    rows = lhs.shape[0]
    step = pl.program_id(0)
    sums = [None, None]
    atom_rows = own_ref.shape[0]
    here = pl.ds(pl.multiple_of(step * rows, rows), rows)
    cos_ref, sin_ref = cos_ref.at[here], sin_ref.at[here]

    @pl.when(step == 0)
    def _():
        begin = pl.multiple_of(places[1], columns.shape[0])
        columns[...] = jnp.transpose(waves_ref[:, pl.ds(begin, columns.shape[0])])
        for number, ref in enumerate((own_pos, other_pos)):
            keep = lax.broadcasted_iota(jnp.int32, ref.shape, 0) < 3
            high, middle, low = thirds(jnp.where(keep, ref[...], jnp.float32(0)))
            rhs[:, number * atom_rows : (number + 1) * atom_rows] = jnp.concatenate(
                [high, middle, high, low, high, middle], axis=0
            ).astype(jnp.bfloat16)

    for part in range(rows // block_rows):
        number = (first + step * (rows // block_rows) + part) ^ places[0]
        at = pl.multiple_of(start + number * block_rows, block_rows)
        turned[part * block_rows : (part + 1) * block_rows, :] = columns[pl.ds(at, block_rows), :]
    high, middle, low = thirds(turned[...])
    lhs[...] = jnp.concatenate([high, high, middle, high, low, middle], axis=1).astype(jnp.bfloat16)

    blocks = [(ref, base) for ref in (own_ref, other_ref) for base in range(0, atom_rows, TILE)]

    def phase(block):
        turns[block % 3] = jnp.dot(
            lhs[...], rhs[:, block * TILE : (block + 1) * TILE], preferred_element_type=jnp.float32
        )

    def fill(block):
        for strip in range(rows // 16):
            at = slice(strip * 16, strip * 16 + 16)
            cos_part, sin_part = cos_sin_turns(turns[block % 3, at, :])
            cos_ref[at, block * TILE : (block + 1) * TILE] = cos_part.astype(jnp.bfloat16)
            sin_ref[at, block * TILE : (block + 1) * TILE] = sin_part.astype(jnp.bfloat16)

    def multiply(block):
        feats_ref, base = blocks[block]
        feats = feats_ref[base : base + TILE, :]
        at = slice(block * TILE, (block + 1) * TILE)
        for which, ref in enumerate((cos_ref, sin_ref)):
            term = jnp.dot(ref[:, at], feats, preferred_element_type=jnp.float32)
            sums[which] = term if sums[which] is None else sums[which] + term

    phase(0)
    for block in range(len(blocks)):
        if block + 1 < len(blocks):
            phase(block + 1)
        fill(block)
        if block > 0:
            multiply(block - 1)
    multiply(len(blocks) - 1)
    for which in range(2):
        sum_ref[which] = sums[which].astype(sum_ref.dtype)


def forward(places, waves, positions, feats, start, position, count, block_rows, dtype):
    depth = waves.shape[0]
    atom_rows, width = feats[0].shape
    tile = min(FORWARD_ROWS, count)
    trig = pltpu.VMEM((count, 2 * atom_rows), jnp.bfloat16)
    return pl.pallas_call(
        functools.partial(forward_body, start, position // block_rows, block_rows),
        grid_spec=pltpu.PrefetchScalarGridSpec(
            num_scalar_prefetch=1,
            grid=(count // tile,),
            in_specs=[
                pl.BlockSpec(array.shape, lambda k, *_: (0, 0), pipeline_mode=pl.Buffered(1))
                for array in (waves, *positions, *feats)
            ],
            out_specs=[
                pl.BlockSpec(memory_space=pltpu.VMEM),
                pl.BlockSpec(memory_space=pltpu.VMEM),
                pl.BlockSpec((2, tile, width), lambda k, *_: (0, k, 0)),
            ],
            scratch_shapes=[
                pltpu.VMEM((waves.shape[1] // 2, depth), jnp.float32),
                pltpu.VMEM((tile, depth), jnp.float32),
                pltpu.VMEM((tile, 6 * depth), jnp.bfloat16),
                pltpu.VMEM((6 * depth, 2 * atom_rows), jnp.bfloat16),
                pltpu.VMEM((3, tile, TILE), jnp.float32),
            ],
        ),
        out_shape=[trig, trig, jax.ShapeDtypeStruct((2, count, width), dtype)],
        compiler_params=LIMIT,
        cost_estimate=pl.CostEstimate(
            flops=18 * count * atom_rows * width,
            transcendentals=0,
            bytes_accessed=8 * count * atom_rows,
        ),
        name="structure",
    )(places, waves, *positions, *feats)


def near_body(base, places, scales, row_ref, left_ref, masked_ref, right_ref, feats_ref, mix_ref, *refs):
    out_ref, wide, kernels, partners = refs[-4:]
    cells_per_step = kernels.shape[0]
    cap = wide.shape[1]
    step = pl.program_id(0)
    kinds = mix_ref.shape[0]
    count = places.shape[1]
    halo = left_ref.shape[0]
    inner = masked_ref.shape[0]

    @pl.when(step == 0)
    def _():
        wide[0:halo] = left_ref[...]
        wide[halo : halo + inner] = masked_ref[...]
        wide[halo + inner :] = right_ref[...]

    for part in range(cells_per_step):
        cell = base + step * cells_per_step + part
        col = jnp.transpose(row_ref[cell + halo])
        for which in range(count):
            place = places[cell, which]
            row = row_ref[place]
            squared = None
            for axis in range(3):
                gap = col[:, axis : axis + 1] - row[axis : axis + 1, :]
                squared = gap * gap if squared is None else squared + gap * gap
            for kind in range(kinds):
                kernels[part, kind * cap : (kind + 1) * cap, which * cap : (which + 1) * cap] = (
                    jnp.exp2(scales[kind] * squared).astype(jnp.bfloat16)
                )
            partners[part, which * cap : (which + 1) * cap, :] = wide[place]
        total = jnp.dot(kernels[part], partners[part], preferred_element_type=jnp.float32)
        at = slice(part * cap, (part + 1) * cap)
        near = feats_ref[at, :].astype(jnp.float32)
        for kind in range(kinds):
            near = near + total[kind * cap : (kind + 1) * cap, :] * mix_ref[kind : kind + 1, :]
        out_ref[at, :] = near


def near_part(base, cells, places, scales, rows, left, masked, right, feats, mix, result):
    count = places.shape[1]
    cap, width = masked.shape[1:]
    kinds = mix.shape[0]
    per = min(4, cells)
    offset = base // per
    args = [] if result is None else [result]
    whole3 = lambda a: pl.BlockSpec(a.shape, lambda c, *_: (0, 0, 0))
    return pl.pallas_call(
        functools.partial(near_body, base),
        grid_spec=pltpu.PrefetchScalarGridSpec(
            num_scalar_prefetch=2,
            grid=(cells // per,),
            in_specs=[
                whole3(rows),
                whole3(left),
                whole3(masked),
                whole3(right),
                pl.BlockSpec((per * cap, width), lambda c, *_: (c + offset, 0)),
                pl.BlockSpec(mix.shape, lambda c, *_: (0, 0)),
            ]
            + [pl.BlockSpec(memory_space=pl.ANY)] * len(args),
            out_specs=pl.BlockSpec((per * cap, width), lambda c, *_: (c + offset, 0)),
            scratch_shapes=[
                pltpu.VMEM((rows.shape[0], cap, width), jnp.bfloat16),
                pltpu.VMEM((per, kinds * cap, count * cap), jnp.bfloat16),
                pltpu.VMEM((per, count * cap, width), jnp.bfloat16),
            ],
        ),
        out_shape=jax.ShapeDtypeStruct(feats.shape, jnp.float32),
        input_output_aliases={8: 0} if args else {},
        cost_estimate=pl.CostEstimate(
            flops=8 * cells * cap * cap * count * width * kinds,
            transcendentals=0,
            bytes_accessed=8 * cells * cap * width,
        ),
        compiler_params=LIMIT,
        name="near",
    )(places, scales, rows, left, masked, right, feats, mix, *args)


def backward_body(parts, first, tile, has_acc, *refs):
    refs = list(refs)
    here = pl.ds(pl.multiple_of(first + pl.program_id(0) * tile, tile), tile)
    trig, filts, rest = refs[: 2 * parts], refs[2 * parts : 3 * parts], refs[3 * parts :]
    contract = (((0,), (0,)), ((), ()))
    total = rest.pop(0)[...] if has_acc else None
    for part in range(parts):
        for which in range(2):
            term = lax.dot_general(
                trig[2 * part + which][:, here],
                filts[part][which],
                contract,
                preferred_element_type=jnp.float32,
            )
            total = term if total is None else total + term
    for ref in rest:
        ref[...] = total.astype(ref.dtype)


def backward(chunks, first, count, tile, acc, dtype):
    parts = [part for chunk in chunks for part in chunk]
    width = parts[0][2].shape[2]
    args, specs = [], []
    if acc is not None:
        offset = acc[1] // tile
        args.append(acc[0])
        specs.append(pl.BlockSpec((tile, width), lambda i: (i + offset, 0)))
    trig = [array for cos, sin, _ in parts for array in (cos, sin)]
    filts = [filt for _, _, filt in parts]
    rows = sum(cos.shape[0] for cos, _, _ in parts)
    return pl.pallas_call(
        functools.partial(backward_body, len(parts), first, tile, acc is not None),
        grid=(count // tile,),
        in_specs=[pl.BlockSpec(memory_space=pltpu.VMEM) for _ in trig]
        + [pl.BlockSpec(filt.shape, lambda i: (0, 0, 0)) for filt in filts]
        + specs,
        out_specs=pl.BlockSpec((tile, width), lambda i: (i, 0)),
        out_shape=jax.ShapeDtypeStruct((count, width), dtype),
        compiler_params=LIMIT,
        cost_estimate=pl.CostEstimate(
            flops=8 * rows * count * width,
            transcendentals=0,
            bytes_accessed=4 * rows * count + 8 * count * width,
        ),
        name="messages",
    )(*trig, *filts, *args)


def mlp_body(side, own_ref, came_ref, other_ref, gain_ref, in_ref, out_ref, both_ref, *refs):
    result_ref = refs[-1]
    width = own_ref.shape[1]
    hidden_count = in_ref.shape[1]
    mine = side[0]
    own = own_ref[...] + came_ref[...].astype(jnp.float32)
    own_wide = own.astype(jnp.bfloat16).astype(jnp.float32)
    other = other_ref[...].astype(jnp.float32)
    mean = (
        jnp.sum(own_wide * own_wide, axis=1, keepdims=True)
        + jnp.sum(other * other, axis=1, keepdims=True)
    ) / (2 * width)
    scale = lax.rsqrt(mean + EPS)
    at_own = pl.ds(pl.multiple_of(mine * width, width), width)
    at_other = pl.ds(pl.multiple_of((1 - mine) * width, width), width)
    normed_own = (own_wide * scale * gain_ref[:, at_own]).astype(jnp.bfloat16)
    normed_other = (other * scale * gain_ref[:, at_other]).astype(jnp.bfloat16)
    total = own
    hidden_columns = slice(0, hidden_count)
    halves = (
        (in_ref.at[:, :], out_ref.at[:, :]),
        (both_ref.at[:, hidden_columns], both_ref.at[:, hidden_count:]),
    )
    for in_half, out_half in halves:
        value = jnp.dot(normed_own, in_half[at_own, :], preferred_element_type=jnp.float32)
        value = value + jnp.dot(
            normed_other, in_half[at_other, :], preferred_element_type=jnp.float32
        )
        half = jnp.float32(0.5) * value
        hidden = (half * jnp.tanh(half) + half).astype(jnp.bfloat16)
        total = total + jnp.dot(hidden, out_half[...], preferred_element_type=jnp.float32)
    result_ref[...] = total.astype(jnp.bfloat16)


def mlp(side, own, came, own_at, other, gains, weights, result, first, total_rows):
    rows, width = other.shape
    offset, own_offset = first // rows, own_at // rows
    args = [] if result is None else [result]
    return pl.pallas_call(
        mlp_body,
        grid_spec=pltpu.PrefetchScalarGridSpec(
            num_scalar_prefetch=1,
            grid=(1,),
            in_specs=[
                pl.BlockSpec((rows, width), lambda i, *_: (own_offset, 0)),
                pl.BlockSpec((rows, width), lambda i, *_: (own_offset, 0)),
                pl.BlockSpec((rows, width), lambda i, *_: (0, 0)),
                pl.BlockSpec(gains.shape, lambda i, *_: (0, 0)),
            ]
            + [pl.BlockSpec(weight.shape, lambda i, *_: (0, 0)) for weight in weights]
            + [pl.BlockSpec(memory_space=pl.ANY)] * len(args),
            out_specs=pl.BlockSpec((rows, width), lambda i, *_: (offset, 0)),
        ),
        out_shape=jax.ShapeDtypeStruct((total_rows, width), jnp.bfloat16),
        input_output_aliases={8: 0} if args else {},
        cost_estimate=pl.CostEstimate(
            flops=2 * rows * width * weights[0].shape[1] * 12,
            transcendentals=0,
            bytes_accessed=8 * rows * width,
        ),
        compiler_params=LIMIT,
        name="mlp",
    )(side, own, came, other, gains, *weights, *args)


def thirds(values):
    def rounded(v):
        return v.astype(jnp.bfloat16).astype(jnp.float32)

    high = rounded(values)
    middle = rounded(values - high)
    return high, middle, values - high - middle


def swap(value):
    return lax.ppermute(value, "waves", [(0, 1), (1, 0)])


def across(value, bit):
    count = lax.axis_size("cells")
    return lax.ppermute(value, "cells", [(i, i ^ bit) for i in range(count)])


def shards(
    features,
    positions,
    occupancy,
    neighbours,
    wavevectors,
    filters,
    falloffs,
    mixing,
    norm_gain,
    in_weight,
    out_weight,
):
    devices = lax.axis_size("cells")
    bits = [1 << b for b in range(devices.bit_length() - 1)]
    core_bit, ring_bits = bits[0], bits[1:]
    group = devices // 2
    cell_count = occupancy.shape[0]
    atom_rows, width = features.shape
    capacity = atom_rows // cell_count
    wave_rows = wavevectors.shape[1]
    all_waves = 2 * wave_rows
    own_waves = wave_rows // 2
    length = jnp.float32(devices * cell_count)
    place = lax.axis_index("cells").astype(jnp.int32)
    side = lax.axis_index("waves").astype(jnp.int32)
    core = place & core_bit

    live = jnp.arange(capacity, dtype=jnp.int32)[None, :, None] < occupancy[:, None, None]
    masked = jnp.where(live, features.reshape(cell_count, capacity, width), jnp.bfloat16(0)).reshape(
        atom_rows, width
    )
    filled = jnp.pad(occupancy.astype(jnp.float32)[None, :], ((0, 4), (0, atom_rows - cell_count)))
    atoms = jnp.concatenate([positions, filled], axis=0)

    pair_feats = (masked, across(masked, core_bit))
    pair_atoms = (atoms, across(atoms, core_bit))

    reverse = jnp.int32(0)
    for index, bit in enumerate(reversed(ring_bits)):
        reverse = reverse | jnp.where((place & bit) != 0, 1 << index, 0).astype(jnp.int32)
    places_of_waves = jnp.stack([reverse, core * own_waves])

    def wave_operand(waves):
        return jnp.pad(waves * jnp.float32(1.0 / (2.0 * math.pi)), ((0, 5), (0, 0)))

    other_waves = swap(wavevectors)

    to_right = [(i, (i + 1) % devices) for i in range(devices)]
    to_left = [((i + 1) % devices, i) for i in range(devices)]
    edge = HW * capacity
    left_feats = lax.ppermute(masked[atom_rows - edge :], "cells", to_right)
    right_feats = lax.ppermute(masked[:edge], "cells", to_left)
    left_pos = lax.ppermute(positions[:, atom_rows - edge :], "cells", to_right)
    right_pos = lax.ppermute(positions[:, :edge], "cells", to_left)
    count = jnp.sum(filled[0, :cell_count] + pair_atoms[1][3, :cell_count])
    count = jnp.full((8, 128), count)
    for bit in ring_bits:
        count = count + across(count, bit)
    count = count[0:1, 0:1]

    def filter_part(start, rows, whose):
        row = core * own_waves + start + reverse * (rows // group)
        return lax.dynamic_slice(filters, (row, whose * width), (rows // group, width))

    unit = 32 * group
    splits = []
    for shares in SHARES:
        begin, pieces_of_half = 0, []
        for share in shares:
            rows_of = max(unit, int(own_waves * share) // unit * unit)
            rows_of = min(rows_of, own_waves - begin)
            if rows_of > 0:
                pieces_of_half.append((begin, rows_of))
            begin += rows_of
        splits.append(pieces_of_half)
    own_filters = [filter_part(start, rows, side) for start, rows in splits[0]]
    sent_filters = jnp.concatenate(
        [filter_part(start, rows, 1 - side) for start, rows in splits[1]], axis=0
    )
    came_filters = swap(sent_filters)
    other_filters = [
        came_filters[start // group : (start + rows) // group] for start, rows in splits[1]
    ]

    hidden_rows = out_weight.shape[0]
    out_own = lax.dynamic_slice(out_weight, (0, side * width), (hidden_rows, width))
    out_sent = lax.dynamic_slice(out_weight, (0, (1 - side) * width), (hidden_rows, width))
    both = swap(jnp.concatenate([in_weight, out_sent], axis=1))

    factor = lax.rsqrt(count) * jnp.float32(1.0 / math.sqrt(all_waves))
    factors = jnp.stack(
        [factor * jnp.float32(WHOLE_COS**-2), factor * jnp.float32(WHOLE_SIN**-2)]
    )

    chunks = []
    for waves, pieces_of_half, filter_rows in (
        (wavevectors, splits[0], own_filters),
        (other_waves, splits[1], other_filters),
    ):
        operand = wave_operand(waves)
        for (start, rows_of), rows_of_filter in zip(pieces_of_half, filter_rows):
            number = len(chunks)
            scaled = lax.optimization_barrier(rows_of_filter[None] * factors)
            half = rows_of // 2
            cos_far, sin_far, send = forward(
                places_of_waves, operand, pair_atoms, pair_feats, start, half, half, rows_of // group, jnp.bfloat16
            )
            cos_near, sin_near, keep = forward(
                places_of_waves, operand, pair_atoms, pair_feats, start, 0, half, rows_of // group, jnp.float32
            )
            for index, bit in enumerate(ring_bits):
                summed = keep + across(send, bit).astype(jnp.float32)
                if index + 1 < len(ring_bits):
                    half = summed.shape[1] // 2
                    keep, send = summed[:, :half], summed[:, half:].astype(jnp.bfloat16)
            filt = (summed * scaled).astype(jnp.bfloat16)
            for index, bit in enumerate(reversed(ring_bits)):
                came = across(filt, bit)
                if index + 1 < len(ring_bits):
                    filt = jnp.concatenate([filt, came], axis=1)
            chunks.append([(cos_near, sin_near, filt), (cos_far, sin_far, came)])

    shift_left = jnp.where(place == 0, length, 0.0).astype(jnp.float32)
    shift_right = jnp.where(place == devices - 1, length, 0.0).astype(jnp.float32)
    first = jnp.array([[1.0], [0.0], [0.0]], jnp.float32)
    wide_pos = jnp.concatenate(
        [left_pos - first * shift_left, positions, right_pos + first * shift_right], axis=1
    )
    rows = jnp.pad(wide_pos, ((0, 5), (0, 0))).reshape(8, cell_count + 2 * HW, capacity).transpose(1, 0, 2)
    places = jnp.arange(cell_count, dtype=jnp.int32)[:, None] + HW + neighbours
    mix = lax.dynamic_slice(mixing, (0, side * width), (mixing.shape[0], width))
    half_cells = cell_count // 2
    half_rows = atom_rows // 2
    mine = None
    for half in range(2):
        mine = near_part(
            half * half_cells,
            half_cells,
            places,
            falloffs * jnp.float32(-1.0 / math.log(2.0)),
            rows,
            left_feats.reshape(HW, capacity, width),
            masked.reshape(cell_count, capacity, width),
            right_feats.reshape(HW, capacity, width),
            features,
            mix,
            mine,
        )

    f32, bf16 = jnp.float32, jnp.bfloat16
    other = None
    at = 0
    for number, size in enumerate(GROUPS):
        taken = chunks[at : at + size] if number + 1 < len(GROUPS) else chunks[at:-1]
        at += size
        if not taken:
            continue
        other = backward(
            taken, atom_rows, atom_rows, half_rows, None if other is None else (other, 0), f32
        )
        mine = backward(taken, 0, atom_rows, half_rows, (mine, 0), f32)
    last = chunks[-1:]
    tile = half_rows // 2
    gains = norm_gain[None, :]
    weights = (in_weight, out_own, both)
    result = None
    for half in range(2):
        send = backward(last, atom_rows + half * half_rows, half_rows, tile, (other, half * half_rows), bf16)
        came = across(send, core_bit)
        part = backward(last, half * half_rows, half_rows, tile, (mine, half * half_rows), f32)
        pieces = 1 if half == 0 else 2
        piece_rows = half_rows // pieces
        for piece in range(pieces):
            rows_of = slice(piece * piece_rows, (piece + 1) * piece_rows)
            arrived = swap((part[rows_of] + came[rows_of].astype(f32)).astype(bf16))
            result = mlp(
                side.reshape(1), part, came, piece * piece_rows, arrived, gains, weights, result,
                half * half_rows + piece * piece_rows, atom_rows,
            )
    return result


def solution(mesh):
    placed = (
        P("cells", "waves"),
        P(None, "cells"),
        P("cells"),
        P("cells", None),
        P(None, "waves"),
        P("waves", None),
        P(),
        P(),
        P(),
        P(None, "waves"),
        P("waves", None),
    )

    return jax.shard_map(
        shards, mesh=mesh, in_specs=placed, out_specs=P("cells", "waves"), check_vma=False
    )
```

```python
import functools
import math

import jax
import jax.numpy as jnp
from jax import lax
from jax.experimental import pallas as pl
from jax.experimental.pallas import tpu as pltpu
from jax.sharding import PartitionSpec as P

EPS = 1e-06
HW = 2
SHARES = ((1.0,), (0.5, 0.5))
GROUPS = (1, 1)
TILE = 256
FORWARD_ROWS = 256
LIMIT = pltpu.CompilerParams(vmem_limit_bytes=8 << 20)

SIN_1, SIN_0, SIN_BY = -8.313817368817206, 20.224572228345814, 12.875426983082301
COS_ROOT, COS_1, COS_0 = 0.9993568028372194, -11.426868481113639, 49.031109066681445
COS_BY = -48.99957374784235
HALF = SIN_BY**2 / 2.0
WHOLE_COS = (SIN_BY * COS_BY) ** 2 / 8.0
WHOLE_SIN = SIN_BY**3 * COS_BY / 8.0


def cos_sin_turns(turns):
    f32 = jnp.float32
    rest = turns - jnp.round(turns)
    square = rest * rest
    sin_quarter = rest * ((square + f32(SIN_1)) * square + f32(SIN_0))
    cos_quarter = (square - f32(COS_ROOT)) * ((square + f32(COS_1)) * square + f32(COS_0))
    sin_half = sin_quarter * cos_quarter
    cos_half = f32(HALF) - sin_quarter * sin_quarter
    return f32(WHOLE_COS) - sin_half * sin_half, sin_half * cos_half


def forward_body(
    start, first, block_rows, places, waves_ref, own_pos, other_pos, own_ref, other_ref,
    cos_ref, sin_ref, sum_ref, columns, turned, lhs, rhs, turns,
):
    rows = lhs.shape[0]
    step = pl.program_id(0)
    sums = [None, None]
    atom_rows = own_ref.shape[0]
    here = pl.ds(pl.multiple_of(step * rows, rows), rows)
    cos_ref, sin_ref = cos_ref.at[here], sin_ref.at[here]

    @pl.when(step == 0)
    def _():
        begin = pl.multiple_of(places[1], columns.shape[0])
        columns[...] = jnp.transpose(waves_ref[:, pl.ds(begin, columns.shape[0])])
        for number, ref in enumerate((own_pos, other_pos)):
            keep = lax.broadcasted_iota(jnp.int32, ref.shape, 0) < 3
            high, middle, low = thirds(jnp.where(keep, ref[...], jnp.float32(0)))
            rhs[:, number * atom_rows : (number + 1) * atom_rows] = jnp.concatenate(
                [high, middle, high, low, high, middle], axis=0
            ).astype(jnp.bfloat16)

    for part in range(rows // block_rows):
        number = (first + step * (rows // block_rows) + part) ^ places[0]
        at = pl.multiple_of(start + number * block_rows, block_rows)
        turned[part * block_rows : (part + 1) * block_rows, :] = columns[pl.ds(at, block_rows), :]
    high, middle, low = thirds(turned[...])
    lhs[...] = jnp.concatenate([high, high, middle, high, low, middle], axis=1).astype(jnp.bfloat16)

    blocks = [(ref, base) for ref in (own_ref, other_ref) for base in range(0, atom_rows, TILE)]

    def phase(block):
        turns[block % 3] = jnp.dot(
            lhs[...], rhs[:, block * TILE : (block + 1) * TILE], preferred_element_type=jnp.float32
        )

    def fill(block):
        for strip in range(rows // 16):
            at = slice(strip * 16, strip * 16 + 16)
            cos_part, sin_part = cos_sin_turns(turns[block % 3, at, :])
            cos_ref[at, block * TILE : (block + 1) * TILE] = cos_part.astype(jnp.bfloat16)
            sin_ref[at, block * TILE : (block + 1) * TILE] = sin_part.astype(jnp.bfloat16)

    def multiply(block):
        feats_ref, base = blocks[block]
        feats = feats_ref[base : base + TILE, :]
        at = slice(block * TILE, (block + 1) * TILE)
        for which, ref in enumerate((cos_ref, sin_ref)):
            term = jnp.dot(ref[:, at], feats, preferred_element_type=jnp.float32)
            sums[which] = term if sums[which] is None else sums[which] + term

    phase(0)
    for block in range(len(blocks)):
        if block + 1 < len(blocks):
            phase(block + 1)
        fill(block)
        if block > 0:
            multiply(block - 1)
    multiply(len(blocks) - 1)
    for which in range(2):
        sum_ref[which] = sums[which].astype(sum_ref.dtype)


def forward(places, waves, positions, feats, start, position, count, block_rows, dtype):
    depth = waves.shape[0]
    atom_rows, width = feats[0].shape
    tile = min(FORWARD_ROWS, count // 2)
    trig = pltpu.VMEM((count, 2 * atom_rows), jnp.bfloat16)
    return pl.pallas_call(
        functools.partial(forward_body, start, position // block_rows, block_rows),
        grid_spec=pltpu.PrefetchScalarGridSpec(
            num_scalar_prefetch=1,
            grid=(count // tile,),
            in_specs=[
                pl.BlockSpec(array.shape, lambda k, *_: (0, 0), pipeline_mode=pl.Buffered(1))
                for array in (waves, *positions, *feats)
            ],
            out_specs=[
                pl.BlockSpec(memory_space=pltpu.VMEM),
                pl.BlockSpec(memory_space=pltpu.VMEM),
                pl.BlockSpec((2, tile, width), lambda k, *_: (0, k, 0)),
            ],
            scratch_shapes=[
                pltpu.VMEM((waves.shape[1] // 2, depth), jnp.float32),
                pltpu.VMEM((tile, depth), jnp.float32),
                pltpu.VMEM((tile, 6 * depth), jnp.bfloat16),
                pltpu.VMEM((6 * depth, 2 * atom_rows), jnp.bfloat16),
                pltpu.VMEM((3, tile, TILE), jnp.float32),
            ],
        ),
        out_shape=[trig, trig, jax.ShapeDtypeStruct((2, count, width), dtype)],
        compiler_params=LIMIT,
        cost_estimate=pl.CostEstimate(
            flops=18 * count * atom_rows * width,
            transcendentals=0,
            bytes_accessed=8 * count * atom_rows,
        ),
        name="structure",
    )(places, waves, *positions, *feats)


def near_body(base, places, scales, row_ref, left_ref, masked_ref, right_ref, feats_ref, mix_ref, *refs):
    out_ref, wide, kernels, partners = refs[-4:]
    cells_per_step = kernels.shape[0]
    cap = wide.shape[1]
    step = pl.program_id(0)
    kinds = mix_ref.shape[0]
    count = places.shape[1]
    halo = left_ref.shape[0]
    inner = masked_ref.shape[0]

    @pl.when(step == 0)
    def _():
        wide[0:halo] = left_ref[...]
        wide[halo : halo + inner] = masked_ref[...]
        wide[halo + inner :] = right_ref[...]

    for part in range(cells_per_step):
        cell = base + step * cells_per_step + part
        col = jnp.transpose(row_ref[cell + halo])
        for which in range(count):
            place = places[cell, which]
            row = row_ref[place]
            squared = None
            for axis in range(3):
                gap = col[:, axis : axis + 1] - row[axis : axis + 1, :]
                squared = gap * gap if squared is None else squared + gap * gap
            for kind in range(kinds):
                kernels[part, kind * cap : (kind + 1) * cap, which * cap : (which + 1) * cap] = (
                    jnp.exp2(scales[kind] * squared).astype(jnp.bfloat16)
                )
            partners[part, which * cap : (which + 1) * cap, :] = wide[place]
        total = jnp.dot(kernels[part], partners[part], preferred_element_type=jnp.float32)
        at = slice(part * cap, (part + 1) * cap)
        near = feats_ref[at, :].astype(jnp.float32)
        for kind in range(kinds):
            near = near + total[kind * cap : (kind + 1) * cap, :] * mix_ref[kind : kind + 1, :]
        out_ref[at, :] = near


def near_part(base, cells, places, scales, rows, left, masked, right, feats, mix, result):
    count = places.shape[1]
    cap, width = masked.shape[1:]
    kinds = mix.shape[0]
    per = min(4, cells)
    offset = base // per
    args = [] if result is None else [result]
    whole3 = lambda a: pl.BlockSpec(a.shape, lambda c, *_: (0, 0, 0))
    return pl.pallas_call(
        functools.partial(near_body, base),
        grid_spec=pltpu.PrefetchScalarGridSpec(
            num_scalar_prefetch=2,
            grid=(cells // per,),
            in_specs=[
                whole3(rows),
                whole3(left),
                whole3(masked),
                whole3(right),
                pl.BlockSpec((per * cap, width), lambda c, *_: (c + offset, 0)),
                pl.BlockSpec(mix.shape, lambda c, *_: (0, 0)),
            ]
            + [pl.BlockSpec(memory_space=pl.ANY)] * len(args),
            out_specs=pl.BlockSpec((per * cap, width), lambda c, *_: (c + offset, 0)),
            scratch_shapes=[
                pltpu.VMEM((rows.shape[0], cap, width), jnp.bfloat16),
                pltpu.VMEM((per, kinds * cap, count * cap), jnp.bfloat16),
                pltpu.VMEM((per, count * cap, width), jnp.bfloat16),
            ],
        ),
        out_shape=jax.ShapeDtypeStruct(feats.shape, jnp.float32),
        input_output_aliases={8: 0} if args else {},
        cost_estimate=pl.CostEstimate(
            flops=8 * cells * cap * cap * count * width * kinds,
            transcendentals=0,
            bytes_accessed=8 * cells * cap * width,
        ),
        compiler_params=LIMIT,
        name="near",
    )(places, scales, rows, left, masked, right, feats, mix, *args)


def backward_body(parts, first, tile, has_acc, *refs):
    refs = list(refs)
    here = pl.ds(pl.multiple_of(first + pl.program_id(0) * tile, tile), tile)
    trig, filts, rest = refs[: 2 * parts], refs[2 * parts : 3 * parts], refs[3 * parts :]
    contract = (((0,), (0,)), ((), ()))
    total = rest.pop(0)[...] if has_acc else None
    for part in range(parts):
        for which in range(2):
            term = lax.dot_general(
                trig[2 * part + which][:, here],
                filts[part][which],
                contract,
                preferred_element_type=jnp.float32,
            )
            total = term if total is None else total + term
    for ref in rest:
        ref[...] = total.astype(ref.dtype)


def backward(chunks, first, count, tile, acc, dtype):
    parts = [part for chunk in chunks for part in chunk]
    width = parts[0][2].shape[2]
    args, specs = [], []
    if acc is not None:
        offset = acc[1] // tile
        args.append(acc[0])
        specs.append(pl.BlockSpec((tile, width), lambda i: (i + offset, 0)))
    trig = [array for cos, sin, _ in parts for array in (cos, sin)]
    filts = [filt for _, _, filt in parts]
    rows = sum(cos.shape[0] for cos, _, _ in parts)
    return pl.pallas_call(
        functools.partial(backward_body, len(parts), first, tile, acc is not None),
        grid=(count // tile,),
        in_specs=[pl.BlockSpec(memory_space=pltpu.VMEM) for _ in trig]
        + [pl.BlockSpec(filt.shape, lambda i: (0, 0, 0)) for filt in filts]
        + specs,
        out_specs=pl.BlockSpec((tile, width), lambda i: (i, 0)),
        out_shape=jax.ShapeDtypeStruct((count, width), dtype),
        compiler_params=LIMIT,
        cost_estimate=pl.CostEstimate(
            flops=8 * rows * count * width,
            transcendentals=0,
            bytes_accessed=4 * rows * count + 8 * count * width,
        ),
        name="messages",
    )(*trig, *filts, *args)


def mlp_body(side, own_ref, came_ref, other_ref, gain_ref, in_ref, out_ref, both_ref, *refs):
    result_ref = refs[-1]
    width = own_ref.shape[1]
    hidden_count = in_ref.shape[1]
    mine = side[0]
    own = own_ref[...] + came_ref[...].astype(jnp.float32)
    own_wide = own.astype(jnp.bfloat16).astype(jnp.float32)
    other = other_ref[...].astype(jnp.float32)
    mean = (
        jnp.sum(own_wide * own_wide, axis=1, keepdims=True)
        + jnp.sum(other * other, axis=1, keepdims=True)
    ) / (2 * width)
    scale = lax.rsqrt(mean + EPS)
    at_own = pl.ds(pl.multiple_of(mine * width, width), width)
    at_other = pl.ds(pl.multiple_of((1 - mine) * width, width), width)
    normed_own = (own_wide * scale * gain_ref[:, at_own]).astype(jnp.bfloat16)
    normed_other = (other * scale * gain_ref[:, at_other]).astype(jnp.bfloat16)
    total = own
    hidden_columns = slice(0, hidden_count)
    halves = (
        (in_ref.at[:, :], out_ref.at[:, :]),
        (both_ref.at[:, hidden_columns], both_ref.at[:, hidden_count:]),
    )
    for in_half, out_half in halves:
        value = jnp.dot(normed_own, in_half[at_own, :], preferred_element_type=jnp.float32)
        value = value + jnp.dot(
            normed_other, in_half[at_other, :], preferred_element_type=jnp.float32
        )
        half = jnp.float32(0.5) * value
        hidden = (half * jnp.tanh(half) + half).astype(jnp.bfloat16)
        total = total + jnp.dot(hidden, out_half[...], preferred_element_type=jnp.float32)
    result_ref[...] = total.astype(jnp.bfloat16)


def mlp(side, own, came, own_at, other, gains, weights, result, first, total_rows):
    rows, width = other.shape
    offset, own_offset = first // rows, own_at // rows
    args = [] if result is None else [result]
    return pl.pallas_call(
        mlp_body,
        grid_spec=pltpu.PrefetchScalarGridSpec(
            num_scalar_prefetch=1,
            grid=(1,),
            in_specs=[
                pl.BlockSpec((rows, width), lambda i, *_: (own_offset, 0)),
                pl.BlockSpec((rows, width), lambda i, *_: (own_offset, 0)),
                pl.BlockSpec((rows, width), lambda i, *_: (0, 0)),
                pl.BlockSpec(gains.shape, lambda i, *_: (0, 0)),
            ]
            + [pl.BlockSpec(weight.shape, lambda i, *_: (0, 0)) for weight in weights]
            + [pl.BlockSpec(memory_space=pl.ANY)] * len(args),
            out_specs=pl.BlockSpec((rows, width), lambda i, *_: (offset, 0)),
        ),
        out_shape=jax.ShapeDtypeStruct((total_rows, width), jnp.bfloat16),
        input_output_aliases={8: 0} if args else {},
        cost_estimate=pl.CostEstimate(
            flops=2 * rows * width * weights[0].shape[1] * 12,
            transcendentals=0,
            bytes_accessed=8 * rows * width,
        ),
        compiler_params=LIMIT,
        name="mlp",
    )(side, own, came, other, gains, *weights, *args)


def thirds(values):
    def rounded(v):
        return v.astype(jnp.bfloat16).astype(jnp.float32)

    high = rounded(values)
    middle = rounded(values - high)
    return high, middle, values - high - middle


def swap(value):
    return lax.ppermute(value, "waves", [(0, 1), (1, 0)])


def across(value, bit):
    count = lax.axis_size("cells")
    return lax.ppermute(value, "cells", [(i, i ^ bit) for i in range(count)])


def shards(
    features,
    positions,
    occupancy,
    neighbours,
    wavevectors,
    filters,
    falloffs,
    mixing,
    norm_gain,
    in_weight,
    out_weight,
):
    devices = lax.axis_size("cells")
    bits = [1 << b for b in range(devices.bit_length() - 1)]
    core_bit, ring_bits = bits[0], bits[1:]
    group = devices // 2
    cell_count = occupancy.shape[0]
    atom_rows, width = features.shape
    capacity = atom_rows // cell_count
    wave_rows = wavevectors.shape[1]
    all_waves = 2 * wave_rows
    own_waves = wave_rows // 2
    length = jnp.float32(devices * cell_count)
    place = lax.axis_index("cells").astype(jnp.int32)
    side = lax.axis_index("waves").astype(jnp.int32)
    core = place & core_bit

    live = jnp.arange(capacity, dtype=jnp.int32)[None, :, None] < occupancy[:, None, None]
    masked = jnp.where(live, features.reshape(cell_count, capacity, width), jnp.bfloat16(0)).reshape(
        atom_rows, width
    )
    filled = jnp.pad(occupancy.astype(jnp.float32)[None, :], ((0, 4), (0, atom_rows - cell_count)))
    atoms = jnp.concatenate([positions, filled], axis=0)

    pair_feats = (masked, across(masked, core_bit))
    pair_atoms = (atoms, across(atoms, core_bit))

    reverse = jnp.int32(0)
    for index, bit in enumerate(reversed(ring_bits)):
        reverse = reverse | jnp.where((place & bit) != 0, 1 << index, 0).astype(jnp.int32)
    places_of_waves = jnp.stack([reverse, core * own_waves])

    def wave_operand(waves):
        return jnp.pad(waves * jnp.float32(1.0 / (2.0 * math.pi)), ((0, 5), (0, 0)))

    other_waves = swap(wavevectors)

    to_right = [(i, (i + 1) % devices) for i in range(devices)]
    to_left = [((i + 1) % devices, i) for i in range(devices)]
    edge = HW * capacity
    left_feats = lax.ppermute(masked[atom_rows - edge :], "cells", to_right)
    right_feats = lax.ppermute(masked[:edge], "cells", to_left)
    left_pos = lax.ppermute(positions[:, atom_rows - edge :], "cells", to_right)
    right_pos = lax.ppermute(positions[:, :edge], "cells", to_left)
    count = jnp.sum(filled[0, :cell_count] + pair_atoms[1][3, :cell_count])
    count = jnp.full((8, 128), count)
    for bit in ring_bits:
        count = count + across(count, bit)
    count = count[0:1, 0:1]

    def filter_part(start, rows, whose):
        row = core * own_waves + start + reverse * (rows // group)
        return lax.dynamic_slice(filters, (row, whose * width), (rows // group, width))

    unit = 16 * group
    splits = []
    for shares in SHARES:
        begin, pieces_of_half = 0, []
        for share in shares:
            rows_of = max(unit, int(own_waves * share) // unit * unit)
            rows_of = min(rows_of, own_waves - begin)
            if rows_of > 0:
                pieces_of_half.append((begin, rows_of))
            begin += rows_of
        splits.append(pieces_of_half)
    own_filters = [filter_part(start, rows, side) for start, rows in splits[0]]
    sent_filters = jnp.concatenate(
        [filter_part(start, rows, 1 - side) for start, rows in splits[1]], axis=0
    )
    came_filters = swap(sent_filters)
    other_filters = [
        came_filters[start // group : (start + rows) // group] for start, rows in splits[1]
    ]

    hidden_rows = out_weight.shape[0]
    out_own = lax.dynamic_slice(out_weight, (0, side * width), (hidden_rows, width))
    out_sent = lax.dynamic_slice(out_weight, (0, (1 - side) * width), (hidden_rows, width))
    both = swap(jnp.concatenate([in_weight, out_sent], axis=1))

    factor = lax.rsqrt(count) * jnp.float32(1.0 / math.sqrt(all_waves))
    factors = jnp.stack(
        [factor * jnp.float32(WHOLE_COS**-2), factor * jnp.float32(WHOLE_SIN**-2)]
    )

    chunks = []
    for waves, pieces_of_half, filter_rows in (
        (wavevectors, splits[0], own_filters),
        (other_waves, splits[1], other_filters),
    ):
        operand = wave_operand(waves)
        for (start, rows_of), rows_of_filter in zip(pieces_of_half, filter_rows):
            number = len(chunks)
            scaled = lax.optimization_barrier(rows_of_filter[None] * factors)
            half = rows_of // 2
            cos_far, sin_far, send = forward(
                places_of_waves, operand, pair_atoms, pair_feats, start, half, half, rows_of // group, jnp.bfloat16
            )
            cos_near, sin_near, keep = forward(
                places_of_waves, operand, pair_atoms, pair_feats, start, 0, half, rows_of // group, jnp.float32
            )
            for index, bit in enumerate(ring_bits):
                summed = keep + across(send, bit).astype(jnp.float32)
                if index + 1 < len(ring_bits):
                    half = summed.shape[1] // 2
                    keep, send = summed[:, :half], summed[:, half:].astype(jnp.bfloat16)
            filt = (summed * scaled).astype(jnp.bfloat16)
            for index, bit in enumerate(reversed(ring_bits)):
                came = across(filt, bit)
                if index + 1 < len(ring_bits):
                    filt = jnp.concatenate([filt, came], axis=1)
            chunks.append([(cos_near, sin_near, filt), (cos_far, sin_far, came)])

    shift_left = jnp.where(place == 0, length, 0.0).astype(jnp.float32)
    shift_right = jnp.where(place == devices - 1, length, 0.0).astype(jnp.float32)
    first = jnp.array([[1.0], [0.0], [0.0]], jnp.float32)
    wide_pos = jnp.concatenate(
        [left_pos - first * shift_left, positions, right_pos + first * shift_right], axis=1
    )
    rows = jnp.pad(wide_pos, ((0, 5), (0, 0))).reshape(8, cell_count + 2 * HW, capacity).transpose(1, 0, 2)
    places = jnp.arange(cell_count, dtype=jnp.int32)[:, None] + HW + neighbours
    mix = lax.dynamic_slice(mixing, (0, side * width), (mixing.shape[0], width))
    half_cells = cell_count // 2
    half_rows = atom_rows // 2
    mine = None
    for half in range(2):
        mine = near_part(
            half * half_cells,
            half_cells,
            places,
            falloffs * jnp.float32(-1.0 / math.log(2.0)),
            rows,
            left_feats.reshape(HW, capacity, width),
            masked.reshape(cell_count, capacity, width),
            right_feats.reshape(HW, capacity, width),
            features,
            mix,
            mine,
        )

    f32, bf16 = jnp.float32, jnp.bfloat16
    other = None
    at = 0
    for number, size in enumerate(GROUPS):
        taken = chunks[at : at + size] if number + 1 < len(GROUPS) else chunks[at:-1]
        at += size
        if not taken:
            continue
        other = backward(
            taken, atom_rows, atom_rows, half_rows, None if other is None else (other, 0), f32
        )
        mine = backward(taken, 0, atom_rows, half_rows, (mine, 0), f32)
    last = chunks[-1:]
    tile = half_rows // 2
    gains = norm_gain[None, :]
    weights = (in_weight, out_own, both)
    result = None
    for half in range(2):
        send = backward(last, atom_rows + half * half_rows, half_rows, tile, (other, half * half_rows), bf16)
        came = across(send, core_bit)
        part = backward(last, half * half_rows, half_rows, tile, (mine, half * half_rows), f32)
        pieces = 1
        piece_rows = half_rows // pieces
        for piece in range(pieces):
            rows_of = slice(piece * piece_rows, (piece + 1) * piece_rows)
            arrived = swap((part[rows_of] + came[rows_of].astype(f32)).astype(bf16))
            result = mlp(
                side.reshape(1), part, came, piece * piece_rows, arrived, gains, weights, result,
                half * half_rows + piece * piece_rows, atom_rows,
            )
    return result


def solution(mesh):
    placed = (
        P("cells", "waves"),
        P(None, "cells"),
        P("cells"),
        P("cells", None),
        P(None, "waves"),
        P("waves", None),
        P(),
        P(),
        P(),
        P(None, "waves"),
        P("waves", None),
    )

    return jax.shard_map(
        shards, mesh=mesh, in_specs=placed, out_specs=P("cells", "waves"), check_vma=False
    )
```
